128 devices in a mesh: tile: 16 (over y, z), layer: 8 (over x, core).
Axes of the slice: x: 4, y: 4, z: 4, core: 2. Of those that a mesh axis runs over, the one named last changes fastest.
Arguments:
- velocity_guess: float32 [2, 128, 3072], P(None, 'tile'), may hold values from -6 to 6
- hardness: float32 [32, 128, 3072], P('layer', 'tile'), may hold values from 0.7 to 1.5
- thickness: float32 [128, 3072], P('tile'), may hold values from 0.5 to 2
- friction: float32 [128, 3072], P('tile'), may hold values from 0.5 to 5
- grounded: int32 [128, 3072], P('tile'), may hold values 0 or 1
- ice_mask: int32 [128, 3072], P('tile'), may hold values 0 or 1
- driving: float32 [2, 128, 3072], P(None, 'tile'), may hold values from -8 to 8
- obs_cell: int32 [16, 8, 16, 512], P('tile', 'layer'), may hold values from 0 to 24575
- obs_east: float32 [16, 8, 16, 512], P('tile', 'layer'), may hold values from -6 to 6
- obs_north: float32 [16, 8, 16, 512], P('tile', 'layer'), may hold values from -6 to 6
- obs_weight: float32 [16, 8, 16, 512], P('tile', 'layer'), may hold values from 0.1 to 1
- obs_count: int32 [16, 8, 16], P('tile', 'layer'), may hold values from 64 to 512, as said below
Outputs:
- velocity: float32 [2, 128, 3072], P(None, 'tile')
- friction_gradient: float32 [128, 3072], P('tile')
The draws below stay inside these ranges and needn't reach their ends.
Inputs may be any that keep to these rules, and one draw needn't show every extreme that they name: `obs_count`: counts lie between 64 and 512; in every draw one destination strip receives full blocks from every device. `obs_cell`: cells are numbered row by row within the destination strip.
All inputs are finite; a program needn't handle non-finite values. No bound on the sum of `grounded` or of `ice_mask` on one device may be relied on, other than what follows from the above.
Results may differ from the reference program's by a relative error of at most 0.00013.
Values sent between devices are 32-bit elements; how exact they have to be, the bound alone decides.
No kernel may reach another device: no remote copies, remote signals or barrier semaphores. Data moves between devices by JAX's collectives and lax.ppermute only.
A program may use at most 64 MiB of HBM per device.

```python
import math
import jax
import jax.numpy as jnp
from jax import lax

CX = 8
NY = 3072
SWEEPS = 40
BLOCK = 512
NX = 128
LAYERS = 32
N_TILE = 16
N_LAYER = 8


def draw_obs_count(key, part):
    first_key, second_key = jax.random.split(jax.random.fold_in(key, 17))
    busiest = jax.random.randint(first_key, (), 0, N_TILE)
    counts = jax.random.randint(second_key, (N_TILE, N_LAYER, N_TILE), BLOCK // 8, BLOCK // 2 + 1)
    target = jnp.arange(N_TILE, dtype=jnp.int32)[None, None, :]
    return jnp.where(target == busiest, BLOCK, counts).astype(jnp.int32)


def plant(entries, own_key, least, top_value):
    longest = entries.shape.index(max(entries.shape))
    spots = []
    for shift in (0, 1):
        where = [jax.random.randint(jax.random.fold_in(own_key, axis), (), 0, length) for axis, length in enumerate(entries.shape)]
        where[longest] = (where[longest] + shift) % entries.shape[longest]
        spots.append(tuple(where))
    return entries.at[spots[0]].set(least).at[spots[1]].set(top_value)


def levels(rng, shape, cuts, low, top_value):
    def one(axis_at, parts):
        draws = jax.random.uniform(jax.random.fold_in(jax.random.fold_in(rng, 6), axis_at), (parts,), jnp.float32, low / len(cuts), top_value / len(cuts))
        return jnp.repeat(jnp.exp(draws), shape[axis_at] // parts).reshape((-1,) + (1,) * (len(shape) - axis_at - 1))

    factor_of = one(*cuts[0])
    for cut in cuts[1:]:
        factor_of = factor_of * one(*cut)
    return factor_of


def bell_draw(stream_key, dims, deviation, bound, cuts=(), held_as=jnp.bfloat16):
    values = deviation * jax.random.normal(stream_key, dims, jnp.float32)
    if cuts:
        values = values * levels(stream_key, dims, cuts, -0.22, 0.18)
    return jnp.clip(values, -bound, bound).astype(held_as)


def setup_inputs(seed: int = 0) -> dict:
    key_of = jax.random.split(jax.random.key(seed), 13)
    return {
        "velocity_guess": bell_draw(key_of[0], (2, NX, NY), 1.0, 6.0, ((1, 16),), jnp.float32),
        "hardness": jnp.clip(jnp.exp(math.log(1.5) - 0.7621401 * jax.random.uniform(key_of[1], (LAYERS, NX, NY), jnp.float32) ** levels(key_of[1], (LAYERS, NX, NY), ((0, 8), (1, 16)), -0.2, 0.2)), 0.7, 1.5),
        "thickness": jnp.clip(0.5 + 1.5 * jax.random.uniform(key_of[2], (NX, NY), jnp.float32) ** levels(key_of[2], (NX, NY), ((0, 16),), -0.2, 0.2), 0.5, 2.0),
        "friction": jnp.clip(jnp.exp(math.log(5.0) - 2.3025851 * jax.random.uniform(key_of[3], (NX, NY), jnp.float32) ** levels(key_of[3], (NX, NY), ((0, 16),), -0.2, 0.2)), 0.5, 5.0),
        "grounded": plant((jax.random.randint(key_of[4], (NX, NY), 0, 10) < 7).astype(jnp.int32), jax.random.fold_in(key_of[4], 1), 0, 1),
        "ice_mask": plant((jax.random.randint(key_of[5], (NX, NY), 0, 10) < 9).astype(jnp.int32), jax.random.fold_in(key_of[5], 1), 0, 1),
        "driving": bell_draw(key_of[6], (2, NX, NY), 2.0, 8.0, ((1, 16),), jnp.float32),
        "obs_cell": plant(jax.random.randint(key_of[7], (N_TILE, N_LAYER, N_TILE, BLOCK), 0, CX * NY), jax.random.fold_in(key_of[7], 1), 0, (CX * NY) - 1).astype(jnp.int32),
        "obs_east": bell_draw(key_of[8], (N_TILE, N_LAYER, N_TILE, BLOCK), 1.0, 6.0, ((0, 16), (1, 8)), jnp.float32),
        "obs_north": bell_draw(key_of[9], (N_TILE, N_LAYER, N_TILE, BLOCK), 1.0, 6.0, ((0, 16), (1, 8)), jnp.float32),
        "obs_weight": jnp.clip(jnp.exp(math.log(1.0) - 2.3025851 * jax.random.uniform(key_of[10], (N_TILE, N_LAYER, N_TILE, BLOCK), jnp.float32) ** levels(key_of[10], (N_TILE, N_LAYER, N_TILE, BLOCK), ((0, 16), (1, 8)), -0.2, 0.2)), 0.1, 1.0),
        "obs_count": draw_obs_count(jax.random.fold_in(key_of[12], 71), 0),
    }


OMEGA = 0.5
REGULAR = 0.01


def pad_cols(field):
    return jnp.pad(field, ((0, 0), (1, 1)))


def pad_rows(field):
    return jnp.pad(field, ((1, 1), (0, 0)))


def col_diff(field):
    wide = pad_cols(field)
    return 0.5 * (wide[:, 2:] - wide[:, :-2])


def row_diff(field):
    return 0.5 * (field[2:] - field[:-2])


def strain_rate(east_vel, north_vel):
    slope_ux = row_diff(east_vel)
    slope_vx = row_diff(north_vel)
    slope_uy = col_diff(east_vel[1:-1])
    slope_vy = col_diff(north_vel[1:-1])
    shear = slope_uy + slope_vx
    return slope_ux * slope_ux + slope_vy * slope_vy + slope_ux * slope_vy + 0.25 * shear * shear + REGULAR


def sweep(east_vel, north_vel, viscous, force_east, force_north, drag, inside):
    centre_visc = viscous[1:-1]
    wide_visc = pad_cols(centre_visc)
    face_north = 0.5 * (centre_visc + viscous[2:])
    face_south = 0.5 * (centre_visc + viscous[:-2])
    face_east = 0.5 * (centre_visc + wide_visc[:, 2:])
    face_west = 0.5 * (centre_visc + wide_visc[:, :-2])
    drag_mid = drag[1:-1]
    inside_mid = inside[1:-1]

    def laplace(field, row_gain, col_gain):
        centre = field[1:-1]
        wide = pad_cols(centre)
        rows_part = face_north * (centre - field[2:]) + face_south * (centre - field[:-2])
        cols_part = face_east * (centre - wide[:, 2:]) + face_west * (centre - wide[:, :-2])
        return row_gain * rows_part + col_gain * cols_part + drag_mid * centre

    cross_east = row_diff(2.0 * viscous * col_diff(north_vel)) + col_diff(centre_visc * row_diff(north_vel))
    cross_north = col_diff(2.0 * centre_visc * row_diff(east_vel)) + row_diff(viscous * col_diff(east_vel))
    resid_east = force_east[1:-1] - (laplace(east_vel, 4.0, 1.0) - cross_east)
    resid_north = force_north[1:-1] - (laplace(north_vel, 1.0, 4.0) - cross_north)
    diag_east = 4.0 * (face_north + face_south) + face_east + face_west + drag_mid + 1.0 - inside_mid
    diag_north = face_north + face_south + 4.0 * (face_east + face_west) + drag_mid + 1.0 - inside_mid
    new_east = inside_mid * (east_vel[1:-1] + OMEGA * resid_east / diag_east)
    new_north = inside_mid * (north_vel[1:-1] + OMEGA * resid_north / diag_north)
    return new_east, new_north


def relax_full(start, forces, viscous, drag, inside):
    visc_pad = pad_rows(viscous)
    drag_pad = pad_rows(drag)
    inside_pad = pad_rows(inside)
    east_force = pad_rows(forces[0])
    north_force = pad_rows(forces[1])

    def one_sweep(step, fields):
        new_east, new_north = sweep(pad_rows(fields[0]), pad_rows(fields[1]), visc_pad, east_force, north_force, drag_pad, inside_pad)
        return jnp.stack([new_east, new_north], 0)

    return lax.fori_loop(0, SWEEPS, one_sweep, start)


def reference(velocity_guess, hardness, thickness, friction, grounded, ice_mask, driving, obs_cell, obs_east, obs_north, obs_weight, obs_count):
    strain = strain_rate(pad_rows(velocity_guess[0]), pad_rows(velocity_guess[1]))
    rate = jnp.power(strain, -1.0 / 3.0)
    viscous = thickness * (0.5 * rate * jnp.sum(hardness, axis=0)) / LAYERS
    drag = friction * grounded.astype(jnp.float32)
    inside = ice_mask.astype(jnp.float32)
    velocity = relax_full(velocity_guess, driving, viscous, drag, inside)
    slots = jnp.arange(BLOCK, dtype=jnp.int32)[None, None, None, :]
    valid = (slots < obs_count[..., None]).astype(jnp.float32)
    weights = (obs_weight * valid).reshape(-1)
    dest = jnp.arange(N_TILE, dtype=jnp.int32)[None, None, :, None]
    cells = (dest * (CX * NY) + obs_cell).reshape(-1).astype(jnp.int32)
    flat_east = velocity[0].reshape(-1)
    flat_north = velocity[1].reshape(-1)
    term_east = weights * (flat_east[cells] - obs_east.reshape(-1))
    term_north = weights * (flat_north[cells] - obs_north.reshape(-1))
    misfit_east = jax.ops.segment_sum(term_east, cells, num_segments=NX * NY).reshape(NX, NY)
    misfit_north = jax.ops.segment_sum(term_north, cells, num_segments=NX * NY).reshape(NX, NY)
    source = jnp.stack([misfit_east, misfit_north], 0)
    adjoint = relax_full(jnp.zeros_like(source), source, viscous, drag, inside)
    gradient = -(drag * (velocity[0] * adjoint[0] + velocity[1] * adjoint[1]))
    return velocity, gradient
```

```python
import jax
import jax.numpy as jnp
from jax import lax
from jax.experimental import pallas as pl
from jax.experimental.pallas import tpu as pltpu
from jax.sharding import PartitionSpec as P

SWEEPS = 40
LAYERS = 32
REGULAR = 0.01

ROWS = 8
COLS = 3072
TILES = COLS // 128
N_TILE = 16
N_LAYER = 8
BLOCK = 512
CHUNK = 24
WIDE = CHUNK + 4 * SWEEPS
NARROW = CHUNK + 2 * SWEEPS
WB = WIDE // 8
NB = NARROW // 8
SHARE = COLS // N_LAYER
F32 = jnp.float32


def lane_iota():
    return lax.broadcasted_iota(jnp.int32, (8, 128), 1)


def lanes_left(x, by):
    by = by % 128
    return pltpu.roll(x, 128 - by, 1) if by else x


def pack_obs_kernel(count_ref, cell_ref, east_ref, north_ref, weight_ref, out_ref):
    row = lax.broadcasted_iota(jnp.int32, (N_TILE, BLOCK), 0)
    slot = lax.broadcasted_iota(jnp.int32, (N_TILE, BLOCK), 1)
    count = jnp.zeros((N_TILE, BLOCK), jnp.int32)
    for d in range(N_TILE):
        count = jnp.where(row == d, count_ref[0, d], count)
    weight = jnp.where(slot < count, weight_ref[...], 0.0)
    cell = cell_ref[...]
    high = cell >> 7
    strip_row = ((cell >> 10) * 11) >> 5
    place = ((high - strip_row * TILES) * ROWS + strip_row) * 128 + (cell & 127)
    out_ref[:, 0:BLOCK] = place.astype(F32)
    out_ref[:, BLOCK : 2 * BLOCK] = weight
    out_ref[:, 2 * BLOCK : 3 * BLOCK] = weight * east_ref[...]
    out_ref[:, 3 * BLOCK : 4 * BLOCK] = weight * north_ref[...]


def layer_windows_kernel(hard_ref, out_ref):
    for g in range(TILES):
        at = slice(128 * g, 128 * g + 128)
        part = (hard_ref[0, :, at] + hard_ref[1, :, at]) + (hard_ref[2, :, at] + hard_ref[3, :, at])
        for dest in range(N_LAYER):
            k = g - (3 * dest - 1)
            if 0 <= k < 5:
                out_ref[dest, :, 128 * k : 128 * k + 128] = part
    out_ref[0, :, 0:128] = jnp.zeros((8, 128), F32)
    out_ref[N_LAYER - 1, :, 512:640] = jnp.zeros((8, 128), F32)


def scatter_kernel(obs_ref, out_ref, lhs_ref, rhs_ref, acc_ref):
    acc_ref[...] = jnp.zeros_like(acc_ref)
    step16 = lax.broadcasted_iota(jnp.int32, (16, BLOCK), 0).astype(F32).astype(jnp.bfloat16)

    def rows(x):
        return jnp.broadcast_to(x, (16, BLOCK)).astype(jnp.bfloat16)

    def body(s, carry):
        place = obs_ref[pl.ds(s, 1), 0:BLOCK].astype(jnp.int32)
        high = rows((place >> 7).astype(F32))
        low = rows((place & 127).astype(F32))
        pieces = []
        for f in range(3):
            value = obs_ref[pl.ds(s, 1), (f + 1) * BLOCK : (f + 2) * BLOCK]
            for _ in range(3):
                piece = value.astype(jnp.bfloat16).astype(F32)
                pieces.append(rows(piece))
                value = value - piece
        zero = jnp.zeros((16, BLOCK), jnp.bfloat16)
        one = jnp.ones((16, BLOCK), jnp.bfloat16)
        for b in range(TILES * ROWS // 16):
            rhs_ref[16 * b : 16 * b + 16, :] = jnp.where(high == step16 + 16.0 * b, one, zero)
        for b in range(8):
            hit = low == step16 + 16.0 * b
            for k in range(9):
                lhs_ref[k * 128 + 16 * b : k * 128 + 16 * b + 16, :] = jnp.where(hit, pieces[k], zero)
        acc_ref[...] += lax.dot_general(
            lhs_ref[...], rhs_ref[...], (((1,), (1,)), ((), ())), preferred_element_type=F32
        )
        return carry

    lax.fori_loop(0, N_TILE, body, 0)
    left = lane_iota() < 64
    zero = jnp.zeros((8, 128), F32)
    for f in range(3):
        total = acc_ref[3 * f * 128 : 3 * f * 128 + 128, :]
        total = total + acc_ref[(3 * f + 1) * 128 : (3 * f + 2) * 128, :]
        total = total + acc_ref[(3 * f + 2) * 128 : (3 * f + 3) * 128, :]
        cells = total.T
        turned = [pltpu.roll(cells[8 * g : 8 * g + 8, :], 64, 1) for g in range(TILES)]
        for dest in range(N_LAYER):
            for k in range(4):
                g = 3 * dest - 1 + k
                a = turned[g] if 0 <= g < TILES else zero
                b = turned[g + 1] if g + 1 < TILES else zero
                out_ref[dest, f, :, 128 * k : 128 * k + 128] = jnp.where(left, a, b)


def map_chunks_kernel(me_ref, part_ref, guess_ref, thick_ref, fric_ref, ground_ref, ice_ref, drive_ref, out_ref):
    first = 3 * me_ref[0] - 1
    lane = lane_iota()
    fields = [[] for _ in range(7)]
    for k in range(5):
        g = first + k
        ok = jnp.logical_and(g >= 0, g < TILES)
        keep = jnp.where(ok, 1.0, 0.0).astype(F32)
        start = pl.multiple_of(jnp.clip(g, 0, TILES - 1) * 128, 128)
        at = pl.ds(start, 128)
        total = part_ref[0, :, 128 * k : 128 * k + 128]
        for src in range(1, N_LAYER):
            total = total + part_ref[src, :, 128 * k : 128 * k + 128]
        fields[0].append(guess_ref[0, :, at] * keep)
        fields[1].append(guess_ref[1, :, at] * keep)
        fields[2].append(thick_ref[:, at] * keep * total)
        fields[3].append(fric_ref[:, at] * ground_ref[:, at].astype(F32) * keep)
        fields[4].append(ice_ref[:, at].astype(F32) * keep)
        fields[5].append(drive_ref[0, :, at] * keep)
        fields[6].append(drive_ref[1, :, at] * keep)
    for t in range(N_TILE):
        a, b = divmod(48 + CHUNK * t, 128)
        tails = []
        for f in range(7):
            x0 = lanes_left(fields[f][a], b)
            x1 = lanes_left(fields[f][a + 1], b)
            x2 = lanes_left(fields[f][a + 2], b) if a + 2 < 5 else x1
            inner = lane < 128 - b
            out_ref[t, f] = jnp.where(inner, x0, x1)
            tails.append(jnp.where(inner, x1, x2))
        for k in range(4):
            tail = tails[2 * k]
            if 2 * k + 1 < 7:
                tail = jnp.where(lane < 56, tail, pltpu.roll(tails[2 * k + 1], 56, 1))
            out_ref[t, 7 + k] = tail


def obs_chunks_kernel(part_ref, out_ref):
    lane = lane_iota()
    for f in range(3):
        sums = []
        for k in range(4):
            total = part_ref[0, f, :, 128 * k : 128 * k + 128]
            for src in range(1, N_LAYER):
                total = total + part_ref[src, f, :, 128 * k : 128 * k + 128]
            sums.append(total)
        for t in range(N_TILE):
            a, b = divmod(24 + CHUNK * t, 128)
            x0 = lanes_left(sums[a], b)
            x1 = lanes_left(sums[a + 1], b) if a + 1 < 4 else x0
            out_ref[t, f] = jnp.where(lane < 128 - b, x0, x1)


def sweeps(coef_ref, gu_ref, gv_ref, u_ref, v_ref, n):
    def around(u, v):
        return (
            u, pltpu.roll(u, 127, 1), pltpu.roll(u, 1, 1),
            v, pltpu.roll(v, 127, 1), pltpu.roll(v, 1, 1),
        )

    def body(_, carry):
        u_first, v_first = u_ref[0], v_ref[0]
        west = around(pltpu.roll(u_ref[n - 1], 1, 0), pltpu.roll(v_ref[n - 1], 1, 0))
        here = around(u_first, v_first)
        for i in range(n):
            if i < n - 1:
                east = around(u_ref[i + 1], v_ref[i + 1])
            else:
                east = around(pltpu.roll(u_first, 7, 0), pltpu.roll(v_first, 7, 0))
            half = coef_ref[0, i]
            for own, other, base, source, ref in ((0, 3, 1, gu_ref, u_ref), (3, 0, 9, gv_ref, v_ref)):
                c = [coef_ref[base + k, i] for k in range(8)]
                a = source[i] + half * here[own]
                b = c[0] * here[own + 1] + c[1] * here[own + 2]
                d = c[2] * east[own] + c[3] * west[own]
                e = c[4] * east[other + 1] + c[5] * west[other + 1]
                g = c[6] * east[other + 2] + c[7] * west[other + 2]
                ref[i] = (a + b) + (d + (e + g))
            west, here = here, east
        return carry

    lax.fori_loop(0, SWEEPS, body, 0)


def forward_kernel(z_ref, u_out, v_out, drag_out, coef_out, flat, blk, nu_ref, coef, u_ref, v_ref, tmp):
    for f in range(7):
        flat[f, 0:128, :] = z_ref[:, f].reshape(128, 128).T
    for k in range(4):
        tail = z_ref[:, 7 + k].reshape(128, 128).T
        flat[2 * k, 128:WIDE, :] = tail[0:56]
        if 2 * k + 1 < 7:
            flat[2 * k + 1, 128:WIDE, :] = tail[56:112]
    for i in range(WB):
        u_ref[i] = flat[0, pl.ds(i, 8, stride=WB), :]
        v_ref[i] = flat[1, pl.ds(i, 8, stride=WB), :]
        for f in range(2, 7):
            blk[f - 2, i] = flat[f, pl.ds(i, 8, stride=WB), :]
    drag_out[...] = flat[3, 2 * SWEEPS : 2 * SWEEPS + CHUNK, :]
    lane = lane_iota()
    up_ok = jnp.where(lane < 127, 1.0, 0.0).astype(F32)
    down_ok = jnp.where(lane > 0, 1.0, 0.0).astype(F32)

    def up(x):
        return pltpu.roll(x, 127, 1) * up_ok

    def down(x):
        return pltpu.roll(x, 1, 1) * down_ok

    def east_of(ref, i):
        return ref[i + 1] if i < WB - 1 else pltpu.roll(ref[0], 7, 0)

    def west_of(ref, i):
        return ref[i - 1] if i > 0 else pltpu.roll(ref[WB - 1], 1, 0)

    for i in range(WB):
        u, v = u_ref[i], v_ref[i]
        ux = 0.5 * (up(u) - down(u))
        vx = 0.5 * (up(v) - down(v))
        uy = 0.5 * (east_of(u_ref, i) - west_of(u_ref, i))
        vy = 0.5 * (east_of(v_ref, i) - west_of(v_ref, i))
        shear = uy + vx
        strain = ux * ux + vy * vy + ux * vy + 0.25 * shear * shear + REGULAR
        rate = jnp.exp(jnp.log(strain) * (-1.0 / 3.0))
        nu_ref[i] = blk[0, i] * (rate * (0.5 / LAYERS))
    for i in range(WB):
        nu = nu_ref[i]
        nu_n, nu_s = up(nu), down(nu)
        nu_e, nu_w = east_of(nu_ref, i), west_of(nu_ref, i)
        drag, inside = blk[1, i], blk[2, i]
        n, s, e, w = 0.5 * (nu + nu_n), 0.5 * (nu + nu_s), 0.5 * (nu + nu_e), 0.5 * (nu + nu_w)
        rest = drag + 1.0 - inside
        q_u = 0.5 * inside / (4.0 * (n + s) + (e + w) + rest)
        q_v = 0.5 * inside / ((n + s) + 4.0 * (e + w) + rest)
        coef[0, i] = 0.5 * inside
        coef[1, i] = 4.0 * q_u * n * up_ok
        coef[2, i] = 4.0 * q_u * s * down_ok
        coef[3, i] = q_u * e
        coef[4, i] = q_u * w
        coef[5, i] = q_u * (0.5 * nu_n + 0.25 * nu_e) * up_ok
        coef[6, i] = -q_u * (0.5 * nu_n + 0.25 * nu_w) * up_ok
        coef[7, i] = -q_u * (0.5 * nu_s + 0.25 * nu_e) * down_ok
        coef[8, i] = q_u * (0.5 * nu_s + 0.25 * nu_w) * down_ok
        coef[9, i] = q_v * n * up_ok
        coef[10, i] = q_v * s * down_ok
        coef[11, i] = 4.0 * q_v * e
        coef[12, i] = 4.0 * q_v * w
        coef[13, i] = q_v * (0.5 * nu_e + 0.25 * nu_n) * up_ok
        coef[14, i] = -q_v * (0.5 * nu_w + 0.25 * nu_n) * up_ok
        coef[15, i] = -q_v * (0.5 * nu_e + 0.25 * nu_s) * down_ok
        coef[16, i] = q_v * (0.5 * nu_w + 0.25 * nu_s) * down_ok
        coef[17, i] = q_u * blk[3, i]
        coef[18, i] = q_v * blk[4, i]
        coef[19, i] = q_u
        coef[20, i] = q_v
    sweeps(coef, coef.at[17], coef.at[18], u_ref, v_ref, WB)
    for k in range(19):
        j = k if k < 17 else k + 2
        for i in range(WB):
            tmp[k % 4, pl.ds(i, 8, stride=WB), :] = coef[j, i]
        for i in range(NB):
            coef_out[k, i] = tmp[k % 4, pl.ds(SWEEPS + i, 8, stride=NB), :]
    for i in range(WB):
        flat[0, pl.ds(i, 8, stride=WB), :] = u_ref[i]
        flat[1, pl.ds(i, 8, stride=WB), :] = v_ref[i]
    u_out[...] = flat[0, SWEEPS : SWEEPS + NARROW, :]
    v_out[...] = flat[1, SWEEPS : SWEEPS + NARROW, :]


def adjoint_kernel(z_ref, u_in, v_in, drag_in, coef, out_ref, flat, u_ref, v_ref, gu_ref, gv_ref, turned):
    weight = z_ref[:, 0].reshape(128, 128).T[0:NARROW]
    flat[0] = weight * u_in[...] - z_ref[:, 1].reshape(128, 128).T[0:NARROW]
    flat[1] = weight * v_in[...] - z_ref[:, 2].reshape(128, 128).T[0:NARROW]
    for i in range(NB):
        gu_ref[i] = coef[17, i] * flat[0, pl.ds(i, 8, stride=NB), :]
        gv_ref[i] = coef[18, i] * flat[1, pl.ds(i, 8, stride=NB), :]
        u_ref[i] = jnp.zeros((8, 128), F32)
        v_ref[i] = jnp.zeros((8, 128), F32)
    sweeps(coef, gu_ref, gv_ref, u_ref, v_ref, NB)
    for i in range(NB):
        flat[0, pl.ds(i, 8, stride=NB), :] = u_ref[i]
        flat[1, pl.ds(i, 8, stride=NB), :] = v_ref[i]
    own = slice(SWEEPS, SWEEPS + CHUNK)
    u, v = u_in[own, :], v_in[own, :]
    turned[0:CHUNK, :] = u
    turned[CHUNK : 2 * CHUNK, :] = v
    turned[2 * CHUNK : 3 * CHUNK, :] = -(drag_in[...] * (u * flat[0, own, :] + v * flat[1, own, :]))
    turned[3 * CHUNK :, :] = jnp.zeros((128 - 3 * CHUNK, 128), F32)
    block = turned[...].T.reshape(N_TILE, 8, 128)
    for layer in range(N_LAYER):
        out_ref[:, layer] = block


def unpack_kernel(z_ref, vel_ref, grad_ref):
    lane = lane_iota()
    for f in range(3):
        for j in range(TILES):
            tile = None
            for chunk in range(128 * j // CHUNK, (128 * j + 127) // CHUNK + 1):
                layer, t = divmod(chunk, N_TILE)
                to = CHUNK * chunk - 128 * j
                piece = lanes_left(z_ref[t, layer], CHUNK * f - to)
                tile = piece if tile is None else jnp.where(lane >= to, piece, tile)
            if f < 2:
                vel_ref[f, :, 128 * j : 128 * j + 128] = tile
            else:
                grad_ref[:, 128 * j : 128 * j + 128] = tile


VMEM = pl.BlockSpec(memory_space=pltpu.VMEM)
SMEM = pl.BlockSpec(memory_space=pltpu.SMEM)


def call(kernel, out_shapes, scratch=(), in_specs=None, flops=0, bytes_accessed=0, **more):
    return pl.pallas_call(
        kernel,
        out_shape=[jax.ShapeDtypeStruct(s, F32) for s in out_shapes],
        in_specs=in_specs,
        out_specs=[VMEM] * len(out_shapes),
        scratch_shapes=list(scratch),
        cost_estimate=pl.CostEstimate(flops=flops, bytes_accessed=bytes_accessed, transcendentals=0),
        **more,
    )


def on_device(
    velocity_guess, hardness, thickness, friction, grounded, ice_mask, driving,
    obs_cell, obs_east, obs_north, obs_weight, obs_count,
):
    slots = (N_TILE, BLOCK)
    (packed,) = call(pack_obs_kernel, [(N_TILE, 4 * BLOCK)], in_specs=[SMEM] + [VMEM] * 4)(
        obs_count.reshape(1, N_TILE), obs_cell.reshape(slots), obs_east.reshape(slots),
        obs_north.reshape(slots), obs_weight.reshape(slots),
    )
    arrived = lax.all_to_all(packed, "tile", split_axis=0, concat_axis=0, tiled=True)
    (parts,) = call(layer_windows_kernel, [(N_LAYER, 8, 640)], in_specs=[VMEM])(hardness)
    parts = lax.all_to_all(parts, "layer", split_axis=0, concat_axis=0, tiled=True)
    (sums,) = call(
        scatter_kernel,
        [(N_LAYER, 3, 8, 512)],
        scratch=[
            pltpu.VMEM((9 * 128, BLOCK), jnp.bfloat16),
            pltpu.VMEM((TILES * ROWS, BLOCK), jnp.bfloat16),
            pltpu.VMEM((9 * 128, TILES * ROWS), F32),
        ],
        in_specs=[VMEM],
        flops=3600000000,
    )(arrived)
    sums = lax.all_to_all(sums, "layer", split_axis=0, concat_axis=0, tiled=True)
    me = lax.axis_index("layer").astype(jnp.int32).reshape(1)
    (maps,) = call(map_chunks_kernel, [(N_TILE, 11, 8, 128)], in_specs=[SMEM] + [VMEM] * 7)(
        me, parts, velocity_guess, thickness, friction, grounded, ice_mask, driving
    )
    maps = lax.all_to_all(maps, "tile", split_axis=0, concat_axis=0, tiled=True)
    (points,) = call(obs_chunks_kernel, [(N_TILE, 3, 8, 128)], in_specs=[VMEM])(sums)
    points = lax.all_to_all(points, "tile", split_axis=0, concat_axis=0, tiled=True)
    wide = (WIDE, 128)
    u, v, drag, coef = call(
        forward_kernel,
        [(NARROW, 128), (NARROW, 128), (CHUNK, 128), (19, NB, 8, 128)],
        scratch=[
            pltpu.VMEM((7,) + wide, F32),
            pltpu.VMEM((5, WB, 8, 128), F32),
            pltpu.VMEM((WB, 8, 128), F32),
            pltpu.VMEM((21, WB, 8, 128), F32),
            pltpu.VMEM((WB, 8, 128), F32),
            pltpu.VMEM((WB, 8, 128), F32),
            pltpu.VMEM((4,) + wide, F32),
        ],
        in_specs=[VMEM],
        flops=3600000000,
    )(maps)
    (shares,) = call(
        adjoint_kernel,
        [(N_TILE, N_LAYER, 8, 128)],
        scratch=[
            pltpu.VMEM((2, NARROW, 128), F32),
            pltpu.VMEM((NB, 8, 128), F32),
            pltpu.VMEM((NB, 8, 128), F32),
            pltpu.VMEM((NB, 8, 128), F32),
            pltpu.VMEM((NB, 8, 128), F32),
            pltpu.VMEM((128, 128), F32),
        ],
        in_specs=[VMEM] * 5,
        flops=3600000000,
    )(points, u, v, drag, coef)
    shares = shares.reshape(N_TILE * N_LAYER, 8, 128)
    shares = lax.all_to_all(shares, ("tile", "layer"), split_axis=0, concat_axis=0, tiled=True)
    velocity, gradient = call(unpack_kernel, [(2, 8, COLS), (8, COLS)], in_specs=[VMEM])(
        shares.reshape(N_TILE, N_LAYER, 8, 128)
    )
    return velocity, gradient


def solution(mesh):
    return jax.shard_map(
        on_device,
        mesh=mesh,
        in_specs=(
            P(None, "tile", None),
            P("layer", "tile", None),
            P("tile", None),
            P("tile", None),
            P("tile", None),
            P("tile", None),
            P(None, "tile", None),
            P("tile", "layer", None, None),
            P("tile", "layer", None, None),
            P("tile", "layer", None, None),
            P("tile", "layer", None, None),
            P("tile", "layer", None),
        ),
        out_specs=(P(None, "tile", None), P("tile", None)),
        check_vma=False,
    )
```

```python
import jax
import jax.numpy as jnp
from jax import lax
from jax.experimental import pallas as pl
from jax.experimental.pallas import tpu as pltpu
from jax.sharding import PartitionSpec as P

SWEEPS = 40
LAYERS = 32
REGULAR = 0.01

ROWS = 8
COLS = 3072
TILES = COLS // 128
N_TILE = 16
N_LAYER = 8
BLOCK = 512
CHUNK = 24
WIDE = CHUNK + 4 * SWEEPS
NARROW = CHUNK + 2 * SWEEPS
WB = WIDE // 8
NB = NARROW // 8
SHARE = COLS // N_LAYER
F32 = jnp.float32
PACK_ROWS = 8 * 11
PIECES = 3
DEPTH = 2048
OBS_ROWS = PACK_ROWS
OBS_AT = 72


def lane_iota():
    return lax.broadcasted_iota(jnp.int32, (8, 128), 1)


def lanes_left(x, by):
    by = by % 128
    return pltpu.roll(x, 128 - by, 1) if by else x


def pack_kernel(
    me_ref, count_ref, cell_ref, east_ref, north_ref, weight_ref,
    guess_ref, fric_ref, ground_ref, ice_ref, drive_ref, out_ref,
):
    row = lax.broadcasted_iota(jnp.int32, (N_TILE, BLOCK), 0)
    slot = lax.broadcasted_iota(jnp.int32, (N_TILE, BLOCK), 1)
    count = jnp.zeros((N_TILE, BLOCK), jnp.int32)
    for d in range(N_TILE):
        count = jnp.where(row == d, count_ref[0, d], count)
    weight = jnp.where(slot < count, weight_ref[...], 0.0)
    cell = cell_ref[...]
    high = cell >> 8
    strip_row = ((cell >> 10) * 11) >> 5
    place = ((high - strip_row * (COLS // 256)) * ROWS + strip_row) * 256 + (cell & 255)
    for f, x in enumerate((place.astype(F32), weight, weight * east_ref[...], weight * north_ref[...])):
        for k in range(4):
            for half in range(2):
                at = pl.ds(8 * half * PACK_ROWS + 8 * 9 + 4 * f + k, 8, stride=PACK_ROWS)
                out_ref[at, :] = x[8 * half : 8 * half + 8, 128 * k : 128 * k + 128]

    first = 3 * me_ref[0] - 1
    lane = lane_iota()
    fields = [[] for _ in range(6)]
    for k in range(5):
        g = first + k
        keep = jnp.where(jnp.logical_and(g >= 0, g < TILES), 1.0, 0.0).astype(F32)
        at = pl.ds(pl.multiple_of(jnp.clip(g, 0, TILES - 1) * 128, 128), 128)
        fields[0].append(guess_ref[0, :, at] * keep)
        fields[1].append(guess_ref[1, :, at] * keep)
        fields[2].append(fric_ref[:, at] * ground_ref[:, at].astype(F32) * keep)
        fields[3].append(ice_ref[:, at].astype(F32) * keep)
        fields[4].append(drive_ref[0, :, at] * keep)
        fields[5].append(drive_ref[1, :, at] * keep)
    for t in range(N_TILE):
        a, b = divmod(48 + CHUNK * t, 128)
        inner = lane < 128 - b
        tails = []
        for f in range(6):
            x0 = lanes_left(fields[f][a], b)
            x1 = lanes_left(fields[f][a + 1], b)
            x2 = lanes_left(fields[f][a + 2], b) if a + 2 < 5 else x1
            out_ref[t * PACK_ROWS + 8 * f : t * PACK_ROWS + 8 * f + 8, :] = jnp.where(inner, x0, x1)
            tails.append(jnp.where(inner, x1, x2))
        for k in range(3):
            at = t * PACK_ROWS + 8 * (6 + k)
            out_ref[at : at + 8, :] = jnp.where(lane < 56, tails[2 * k], pltpu.roll(tails[2 * k + 1], 56, 1))


def stiffness_kernel(hard_ref, thick_ref, out_ref):
    for g in range(TILES):
        at = slice(128 * g, 128 * g + 128)
        part = (hard_ref[0, :, at] + hard_ref[1, :, at]) + (hard_ref[2, :, at] + hard_ref[3, :, at])
        out_ref[:, at] = thick_ref[:, at] * part


def scatter_kernel(obs_ref, stiff_ref, out_ref, lhs_ref, rhs_ref, acc_ref):
    acc_ref[...] = jnp.zeros_like(acc_ref)
    step16 = lax.broadcasted_iota(jnp.int32, (16, 128), 0).astype(F32).astype(jnp.bfloat16)
    zero16 = jnp.zeros((16, 128), jnp.bfloat16)
    one16 = jnp.ones((16, 128), jnp.bfloat16)

    def rows(x):
        return jnp.broadcast_to(x, (16, 128)).astype(jnp.bfloat16)

    def body(step, carry):
        for q in range(DEPTH // 128):
            lanes = slice(128 * q, 128 * q + 128)
            base = (step * (DEPTH // BLOCK) + q // 4) * OBS_ROWS + OBS_AT + q % 4
            place = obs_ref[pl.ds(base, 1), :].astype(jnp.int32)
            high = rows((place >> 8).astype(F32))
            low = rows((place & 255).astype(F32))
            pieces = []
            for f in range(3):
                value = obs_ref[pl.ds(base + 4 * (f + 1), 1), :]
                for k in range(PIECES):
                    piece = value.astype(jnp.bfloat16).astype(F32)
                    pieces.append(rows(piece))
                    if k < PIECES - 1:
                        value = value - piece
            for b in range(16):
                rhs_ref[16 * b : 16 * b + 16, lanes] = jnp.where(low == step16 + 16.0 * b, one16, zero16)
            for b in range(6):
                hit = high == step16 + 16.0 * b
                for k in range(3 * PIECES):
                    lhs_ref[k * 96 + 16 * b : k * 96 + 16 * b + 16, lanes] = jnp.where(hit, pieces[k], zero16)
        acc_ref[...] += lax.dot_general(
            lhs_ref[...], rhs_ref[...], (((1,), (1,)), ((), ())), preferred_element_type=F32
        )
        return carry

    lax.fori_loop(0, N_TILE * BLOCK // DEPTH, body, 0)
    lane = lane_iota()
    zero = jnp.zeros((8, 128), F32)

    def windows(tiles, shift, count):
        turned = [lanes_left(x, shift) for x in tiles]
        pick = lambda g: turned[g] if 0 <= g < TILES else zero
        return [
            [jnp.where(lane < 128 - shift, pick(3 * dest - 1 + k), pick(3 * dest + k)) for k in range(count)]
            for dest in range(N_LAYER)
        ]

    stiff = windows([stiff_ref[:, 128 * g : 128 * g + 128] for g in range(TILES)], 48, 5)
    for f in range(3):
        total = acc_ref[PIECES * f * 96 : PIECES * f * 96 + 96, :]
        for k in range(1, PIECES):
            total = total + acc_ref[(PIECES * f + k) * 96 : (PIECES * f + k + 1) * 96, :]
        tiles = [total[8 * (g // 2) : 8 * (g // 2) + 8, 128 * (g % 2) : 128 * (g % 2) + 128] for g in range(TILES)]
        sums = windows(tiles, 88, 4)
        for dest in range(N_LAYER):
            for k in range(4):
                tile = sums[dest][k]
                if f == 0 and k == 3:
                    tile = jnp.where(lane < 80, tile, pltpu.roll(stiff[dest][4], 80, 1))
                out_ref[dest, 4 + 4 * f + k] = tile
    for dest in range(N_LAYER):
        for k in range(4):
            out_ref[dest, k] = stiff[dest][k]


def chunks_kernel(part_ref, out_ref):
    lane = lane_iota()

    def summed(k):
        total = part_ref[0, k]
        for src in range(1, N_LAYER):
            total = total + part_ref[src, k]
        return total

    tiles = [summed(k) for k in range(16)]
    stiff = tiles[0:4] + [lanes_left(tiles[7], 80)]
    for t in range(N_TILE):
        a, b = divmod(CHUNK * t, 128)
        inner = lane < 128 - b
        for f in range(4):
            x = stiff if f == 0 else tiles[4 * f : 4 * f + 4]
            x0 = lanes_left(x[a], b)
            x1 = lanes_left(x[a + 1], b) if a + 1 < len(x) else x0
            out_ref[t, f] = jnp.where(inner, x0, x1)
            if f == 0:
                x2 = lanes_left(x[a + 2], b) if a + 2 < 5 else x1
                out_ref[t, 4] = jnp.where(inner, x1, x2)


def put_state(ref, i, u, v):
    for at, x in ((0, u), (3, v)):
        ref[at, i] = x
        ref[at + 1, i] = pltpu.roll(x, 127, 1)
        ref[at + 2, i] = pltpu.roll(x, 1, 1)


def sweep(coef_ref, gu_ref, gv_ref, old, new, n, start):
    def west_side(i):
        return [old[k, i - 1] if i > 0 else pltpu.roll(old[k, n - 1], 1, 0) for k in range(6)]

    west = west_side(start)
    here = [old[k, start] for k in range(6)]
    for step in range(n):
        i = (start + step) % n
        if step and i == 0:
            west = west_side(0)
            here = [old[k, 0] for k in range(6)]
        east = [old[k, i + 1] if i < n - 1 else pltpu.roll(old[k, 0], 7, 0) for k in range(6)]
        half = coef_ref[0, i]
        fresh = []
        for own, other, base, source in ((0, 3, 1, gu_ref), (3, 0, 9, gv_ref)):
            c = [coef_ref[base + k, i] for k in range(8)]
            a = source[i] + half * here[own]
            b = c[0] * here[own + 1] + c[1] * here[own + 2]
            d = c[2] * east[own] + c[3] * west[own]
            e = c[4] * east[other + 1] + c[5] * west[other + 1]
            g = c[6] * east[other + 2] + c[7] * west[other + 2]
            fresh.append((a + b) + (d + (e + g)))
        put_state(new, i, *fresh)
        west, here = here, east


def sweeps(coef_ref, gu_ref, gv_ref, one, two, n):
    def body(_, carry):
        sweep(coef_ref, gu_ref, gv_ref, one, two, n, 0)
        sweep(coef_ref, gu_ref, gv_ref, two, one, n, n // 2)
        return carry

    lax.fori_loop(0, SWEEPS // 2, body, 0)


def up_down():
    lane = lane_iota()
    up_ok = jnp.where(lane < 127, 1.0, 0.0).astype(F32)
    down_ok = jnp.where(lane > 0, 1.0, 0.0).astype(F32)
    return up_ok, down_ok, lambda x: pltpu.roll(x, 127, 1) * up_ok, lambda x: pltpu.roll(x, 1, 1) * down_ok


def east_of(ref, i):
    return ref[i + 1] if i < WB - 1 else pltpu.roll(ref[0], 7, 0)


def west_of(ref, i):
    return ref[i - 1] if i > 0 else pltpu.roll(ref[WB - 1], 1, 0)


def prepare_kernel(x_ref, blk, flat):
    def tile(k):
        return jnp.concatenate(
            [x_ref[t * PACK_ROWS + 8 * k : t * PACK_ROWS + 8 * k + 8, :] for t in range(N_TILE)], 0
        ).T

    for f in range(6):
        flat[f, 0:128, :] = tile(f)
    for k in range(3):
        tail = tile(6 + k)
        flat[2 * k, 128:WIDE, :] = tail[0:56]
        flat[2 * k + 1, 128:WIDE, :] = tail[56:112]
    for f in range(6):
        for i in range(WB):
            blk[f, i] = flat[f, pl.ds(i, 8, stride=WB), :]
    _, _, up, down = up_down()
    u_ref, v_ref = blk.at[0], blk.at[1]
    for i in range(WB):
        u, v = u_ref[i], v_ref[i]
        ux = 0.5 * (up(u) - down(u))
        vx = 0.5 * (up(v) - down(v))
        uy = 0.5 * (east_of(u_ref, i) - west_of(u_ref, i))
        vy = 0.5 * (east_of(v_ref, i) - west_of(v_ref, i))
        shear = uy + vx
        strain = ux * ux + vy * vy + ux * vy + 0.25 * shear * shear + REGULAR
        blk[6, i] = jnp.exp(jnp.log(strain) * (-1.0 / 3.0)) * (0.5 / LAYERS)


def solve_kernel(
    z_ref, blk, out_ref, flat, nu_ref, coef, wide_a, wide_b, tmp, near, near_a, near_b, gu_ref, gv_ref, turned
):
    def tile(k):
        return z_ref[:, k].reshape(128, 128).T

    flat[0, 0:128, :] = tile(0)
    flat[0, 128:WIDE, :] = tile(4)[0:56]
    up_ok, down_ok, up, down = up_down()
    for i in range(WB):
        put_state(wide_a, i, blk[0, i], blk[1, i])
        nu_ref[i] = blk[6, i] * flat[0, pl.ds(i, 8, stride=WB), :]
    for i in range(WB):
        nu = nu_ref[i]
        nu_n, nu_s = up(nu), down(nu)
        nu_e, nu_w = east_of(nu_ref, i), west_of(nu_ref, i)
        drag, inside = blk[2, i], blk[3, i]
        n, s, e, w = 0.5 * (nu + nu_n), 0.5 * (nu + nu_s), 0.5 * (nu + nu_e), 0.5 * (nu + nu_w)
        rest = drag + 1.0 - inside
        q_u = 0.5 * inside / (4.0 * (n + s) + (e + w) + rest)
        q_v = 0.5 * inside / ((n + s) + 4.0 * (e + w) + rest)
        coef[0, i] = 0.5 * inside
        coef[1, i] = 4.0 * q_u * n * up_ok
        coef[2, i] = 4.0 * q_u * s * down_ok
        coef[3, i] = q_u * e
        coef[4, i] = q_u * w
        coef[5, i] = q_u * (0.5 * nu_n + 0.25 * nu_e) * up_ok
        coef[6, i] = -q_u * (0.5 * nu_n + 0.25 * nu_w) * up_ok
        coef[7, i] = -q_u * (0.5 * nu_s + 0.25 * nu_e) * down_ok
        coef[8, i] = q_u * (0.5 * nu_s + 0.25 * nu_w) * down_ok
        coef[9, i] = q_v * n * up_ok
        coef[10, i] = q_v * s * down_ok
        coef[11, i] = 4.0 * q_v * e
        coef[12, i] = 4.0 * q_v * w
        coef[13, i] = q_v * (0.5 * nu_e + 0.25 * nu_n) * up_ok
        coef[14, i] = -q_v * (0.5 * nu_w + 0.25 * nu_n) * up_ok
        coef[15, i] = -q_v * (0.5 * nu_e + 0.25 * nu_s) * down_ok
        coef[16, i] = q_v * (0.5 * nu_w + 0.25 * nu_s) * down_ok
        coef[17, i] = q_u * blk[4, i]
        coef[18, i] = q_v * blk[5, i]
        coef[19, i] = q_u
        coef[20, i] = q_v
    for k in range(19):
        j = k if k < 17 else k + 2
        for i in range(WB):
            tmp[k % 4, pl.ds(i, 8, stride=WB), :] = coef[j, i]
        for i in range(NB):
            near[k, i] = tmp[k % 4, pl.ds(SWEEPS + i, 8, stride=NB), :]
    sweeps(coef, coef.at[17], coef.at[18], wide_a, wide_b, WB)
    for i in range(WB):
        flat[0, pl.ds(i, 8, stride=WB), :] = wide_a[0, i]
        flat[1, pl.ds(i, 8, stride=WB), :] = wide_a[3, i]
        flat[2, pl.ds(i, 8, stride=WB), :] = blk[2, i]
    weight = tile(1)[0:NARROW]
    span = slice(SWEEPS, SWEEPS + NARROW)
    tmp[0, 0:NARROW, :] = weight * flat[0, span, :] - tile(2)[0:NARROW]
    tmp[1, 0:NARROW, :] = weight * flat[1, span, :] - tile(3)[0:NARROW]
    for i in range(NB):
        gu_ref[i] = near[17, i] * tmp[0, pl.ds(i, 8, stride=NB), :]
        gv_ref[i] = near[18, i] * tmp[1, pl.ds(i, 8, stride=NB), :]
        for k in range(6):
            near_a[k, i] = jnp.zeros((8, 128), F32)
    sweeps(near, gu_ref, gv_ref, near_a, near_b, NB)
    for i in range(NB):
        tmp[0, pl.ds(i, 8, stride=NB), :] = near_a[0, i]
        tmp[1, pl.ds(i, 8, stride=NB), :] = near_a[3, i]
    own = slice(2 * SWEEPS, 2 * SWEEPS + CHUNK)
    mine = slice(SWEEPS, SWEEPS + CHUNK)
    u, v, drag = flat[0, own, :], flat[1, own, :], flat[2, own, :]
    turned[0:CHUNK, :] = u
    turned[CHUNK : 2 * CHUNK, :] = v
    turned[2 * CHUNK : 3 * CHUNK, :] = -(drag * (u * tmp[0, mine, :] + v * tmp[1, mine, :]))
    turned[3 * CHUNK :, :] = jnp.zeros((128 - 3 * CHUNK, 128), F32)
    block = turned[...].T.reshape(N_TILE, 8, 128)
    for layer in range(N_LAYER):
        out_ref[:, layer] = block


def unpack_kernel(z_ref, vel_ref, grad_ref):
    lane = lane_iota()
    for f in range(3):
        for j in range(TILES):
            tile = None
            for chunk in range(128 * j // CHUNK, (128 * j + 127) // CHUNK + 1):
                layer, t = divmod(chunk, N_TILE)
                to = CHUNK * chunk - 128 * j
                piece = lanes_left(z_ref[t, layer], CHUNK * f - to)
                tile = piece if tile is None else jnp.where(lane >= to, piece, tile)
            if f < 2:
                vel_ref[f, :, 128 * j : 128 * j + 128] = tile
            else:
                grad_ref[:, 128 * j : 128 * j + 128] = tile


VMEM = pl.BlockSpec(memory_space=pltpu.VMEM)
SMEM = pl.BlockSpec(memory_space=pltpu.SMEM)


def call(kernel, out_shapes, scratch=(), in_specs=None, flops=1000000, limit=8):
    return pl.pallas_call(
        kernel,
        out_shape=[jax.ShapeDtypeStruct(s, F32) for s in out_shapes],
        in_specs=in_specs,
        out_specs=[VMEM] * len(out_shapes),
        scratch_shapes=list(scratch),
        cost_estimate=pl.CostEstimate(flops=flops, bytes_accessed=1000000, transcendentals=0),
        compiler_params=pltpu.CompilerParams(vmem_limit_bytes=limit << 20),
    )


def exchange(x, axis):
    return lax.all_to_all(x, axis, split_axis=0, concat_axis=0, tiled=True)


def on_device(
    velocity_guess, hardness, thickness, friction, grounded, ice_mask, driving,
    obs_cell, obs_east, obs_north, obs_weight, obs_count,
):
    slots = (N_TILE, BLOCK)
    me = lax.axis_index("layer").astype(jnp.int32).reshape(1)
    (packed,) = call(pack_kernel, [(N_TILE * PACK_ROWS, 128)], in_specs=[SMEM] * 2 + [VMEM] * 9, limit=58)(
        me, obs_count.reshape(1, N_TILE), obs_cell.reshape(slots), obs_east.reshape(slots),
        obs_north.reshape(slots), obs_weight.reshape(slots),
        velocity_guess, friction, grounded, ice_mask, driving,
    )
    arrived = exchange(packed.reshape(N_TILE, PACK_ROWS, 128), "tile").reshape(N_TILE * PACK_ROWS, 128)
    (stiff,) = call(stiffness_kernel, [(8, COLS)], in_specs=[VMEM] * 2)(hardness, thickness)
    (parts,) = call(
        scatter_kernel,
        [(N_LAYER, 16, 8, 128)],
        scratch=[
            pltpu.VMEM((3 * PIECES * 96, DEPTH), jnp.bfloat16),
            pltpu.VMEM((256, DEPTH), jnp.bfloat16),
            pltpu.VMEM((3 * PIECES * 96, 256), F32),
        ],
        in_specs=[VMEM] * 2,
        flops=3600000000,
        limit=16,
    )(arrived, stiff)
    parts = exchange(parts, "layer")
    (blocks,) = call(
        prepare_kernel, [(7, WB, 8, 128)], scratch=[pltpu.VMEM((6, WIDE, 128), F32)], in_specs=[VMEM]
    )(arrived)
    (chunks,) = call(chunks_kernel, [(N_TILE, 5, 8, 128)], in_specs=[VMEM])(parts)
    chunks = exchange(chunks, "tile")
    (shares,) = call(
        solve_kernel,
        [(N_TILE, N_LAYER, 8, 128)],
        scratch=[
            pltpu.VMEM((3, WIDE, 128), F32),
            pltpu.VMEM((WB, 8, 128), F32),
            pltpu.VMEM((21, WB, 8, 128), F32),
            pltpu.VMEM((6, WB, 8, 128), F32),
            pltpu.VMEM((6, WB, 8, 128), F32),
            pltpu.VMEM((4, WIDE, 128), F32),
            pltpu.VMEM((19, NB, 8, 128), F32),
            pltpu.VMEM((6, NB, 8, 128), F32),
            pltpu.VMEM((6, NB, 8, 128), F32),
            pltpu.VMEM((NB, 8, 128), F32),
            pltpu.VMEM((NB, 8, 128), F32),
            pltpu.VMEM((128, 128), F32),
        ],
        in_specs=[VMEM] * 2,
        flops=3600000000,
        limit=16,
    )(chunks, blocks)
    shares = exchange(shares.reshape(N_TILE * N_LAYER, 8, 128), ("tile", "layer"))
    velocity, gradient = call(unpack_kernel, [(2, 8, COLS), (8, COLS)], in_specs=[VMEM])(
        shares.reshape(N_TILE, N_LAYER, 8, 128)
    )
    return velocity, gradient


def solution(mesh):
    return jax.shard_map(
        on_device,
        mesh=mesh,
        in_specs=(
            P(None, "tile", None),
            P("layer", "tile", None),
            P("tile", None),
            P("tile", None),
            P("tile", None),
            P("tile", None),
            P(None, "tile", None),
            P("tile", "layer", None, None),
            P("tile", "layer", None, None),
            P("tile", "layer", None, None),
            P("tile", "layer", None, None),
            P("tile", "layer", None),
        ),
        out_specs=(P(None, "tile", None), P("tile", None)),
        check_vma=False,
    )
```

```python
import jax
import jax.numpy as jnp
from jax import lax
from jax.experimental import pallas as pl
from jax.experimental.pallas import tpu as pltpu
from jax.sharding import PartitionSpec as P

SWEEPS = 40
LAYERS = 32
REGULAR = 0.01

ROWS = 8
COLS = 3072
TILES = COLS // 128
N_TILE = 16
N_LAYER = 8
BLOCK = 512
CHUNK = 24
WIDE = CHUNK + 4 * SWEEPS
NARROW = CHUNK + 2 * SWEEPS
WB = WIDE // 8
NB = NARROW // 8
SHARE = COLS // N_LAYER
F32 = jnp.float32
PACK_ROWS = 8 * 11
PIECES = 3
DEPTH = 2048
OBS_ROWS = PACK_ROWS
OBS_AT = 72


def lane_iota():
    return lax.broadcasted_iota(jnp.int32, (8, 128), 1)


def lanes_left(x, by):
    by = by % 128
    return pltpu.roll(x, 128 - by, 1) if by else x


def pack_kernel(
    me_ref, count_ref, cell_ref, east_ref, north_ref, weight_ref,
    guess_ref, fric_ref, ground_ref, ice_ref, drive_ref, out_ref,
):
    row = lax.broadcasted_iota(jnp.int32, (N_TILE, BLOCK), 0)
    slot = lax.broadcasted_iota(jnp.int32, (N_TILE, BLOCK), 1)
    count = jnp.zeros((N_TILE, BLOCK), jnp.int32)
    for d in range(N_TILE):
        count = jnp.where(row == d, count_ref[0, d], count)
    weight = jnp.where(slot < count, weight_ref[...], 0.0)
    cell = cell_ref[...]
    high = cell >> 8
    strip_row = ((cell >> 10) * 11) >> 5
    place = ((high - strip_row * (COLS // 256)) * ROWS + strip_row) * 256 + (cell & 255)
    for f, x in enumerate((place.astype(F32), weight, weight * east_ref[...], weight * north_ref[...])):
        for k in range(4):
            for half in range(2):
                at = pl.ds(8 * half * PACK_ROWS + 8 * 9 + 4 * f + k, 8, stride=PACK_ROWS)
                out_ref[at, :] = x[8 * half : 8 * half + 8, 128 * k : 128 * k + 128]

    first = 3 * me_ref[0] - 1
    lane = lane_iota()
    fields = [[] for _ in range(6)]
    for k in range(5):
        g = first + k
        keep = jnp.where(jnp.logical_and(g >= 0, g < TILES), 1.0, 0.0).astype(F32)
        at = pl.ds(pl.multiple_of(jnp.clip(g, 0, TILES - 1) * 128, 128), 128)
        fields[0].append(guess_ref[0, :, at] * keep)
        fields[1].append(guess_ref[1, :, at] * keep)
        fields[2].append(fric_ref[:, at] * ground_ref[:, at].astype(F32) * keep)
        fields[3].append(ice_ref[:, at].astype(F32) * keep)
        fields[4].append(drive_ref[0, :, at] * keep)
        fields[5].append(drive_ref[1, :, at] * keep)
    for t in range(N_TILE):
        a, b = divmod(48 + CHUNK * t, 128)
        inner = lane < 128 - b
        tails = []
        for f in range(6):
            x0 = lanes_left(fields[f][a], b)
            x1 = lanes_left(fields[f][a + 1], b)
            x2 = lanes_left(fields[f][a + 2], b) if a + 2 < 5 else x1
            out_ref[t * PACK_ROWS + 8 * f : t * PACK_ROWS + 8 * f + 8, :] = jnp.where(inner, x0, x1)
            tails.append(jnp.where(inner, x1, x2))
        for k in range(3):
            at = t * PACK_ROWS + 8 * (6 + k)
            out_ref[at : at + 8, :] = jnp.where(lane < 56, tails[2 * k], pltpu.roll(tails[2 * k + 1], 56, 1))


def stiffness_kernel(hard_ref, thick_ref, out_ref):
    for g in range(TILES):
        at = slice(128 * g, 128 * g + 128)
        part = (hard_ref[0, :, at] + hard_ref[1, :, at]) + (hard_ref[2, :, at] + hard_ref[3, :, at])
        out_ref[:, at] = thick_ref[:, at] * part


def scatter_kernel(me_ref, obs_ref, stiff_ref, *refs):
    outs, (lhs_ref, rhs_ref, acc_ref, turned_ref) = refs[:N_LAYER], refs[N_LAYER:]
    acc_ref[...] = jnp.zeros_like(acc_ref)
    step16 = lax.broadcasted_iota(jnp.int32, (16, 128), 0).astype(F32).astype(jnp.bfloat16)
    zero16 = jnp.zeros((16, 128), jnp.bfloat16)
    one16 = jnp.ones((16, 128), jnp.bfloat16)

    def rows(x):
        return jnp.broadcast_to(x, (16, 128)).astype(jnp.bfloat16)

    def body(step, carry):
        for q in range(DEPTH // 128):
            lanes = slice(128 * q, 128 * q + 128)
            base = (step * (DEPTH // BLOCK) + q // 4) * OBS_ROWS + OBS_AT + q % 4
            place = obs_ref[pl.ds(base, 1), :].astype(jnp.int32)
            high = rows((place >> 8).astype(F32))
            low = rows((place & 255).astype(F32))
            pieces = []
            for f in range(3):
                value = obs_ref[pl.ds(base + 4 * (f + 1), 1), :]
                for k in range(PIECES):
                    piece = value.astype(jnp.bfloat16).astype(F32)
                    pieces.append(rows(piece))
                    if k < PIECES - 1:
                        value = value - piece
            for b in range(16):
                rhs_ref[16 * b : 16 * b + 16, lanes] = jnp.where(low == step16 + 16.0 * b, one16, zero16)
            for b in range(6):
                hit = high == step16 + 16.0 * b
                for k in range(3 * PIECES):
                    lhs_ref[k * 96 + 16 * b : k * 96 + 16 * b + 16, lanes] = jnp.where(hit, pieces[k], zero16)
        acc_ref[...] += lax.dot_general(
            lhs_ref[...], rhs_ref[...], (((1,), (1,)), ((), ())), preferred_element_type=F32
        )
        return carry

    lax.fori_loop(0, N_TILE * BLOCK // DEPTH, body, 0)
    lane = lane_iota()
    zero = jnp.zeros((8, 128), F32)

    def turn(f, tiles, shift):
        turned = [zero] + [lanes_left(x, shift) for x in tiles] + [zero, zero]
        for g in range(TILES + 2):
            turned_ref[f, g] = jnp.where(lane < 128 - shift, turned[g], turned[g + 1])

    turn(0, [stiff_ref[:, 128 * g : 128 * g + 128] for g in range(TILES)], 48)
    for f in range(3):
        total = acc_ref[PIECES * f * 96 : PIECES * f * 96 + 96, :]
        for k in range(1, PIECES):
            total = total + acc_ref[(PIECES * f + k) * 96 : (PIECES * f + k + 1) * 96, :]
        tiles = [total[8 * (g // 2) : 8 * (g // 2) + 8, 128 * (g % 2) : 128 * (g % 2) + 128] for g in range(TILES)]
        turn(f + 1, tiles, 88)
    for d in range(N_LAYER):
        first = 3 * ((me_ref[0] + d) & (N_LAYER - 1))
        for f in range(4):
            for k in range(4):
                tile = turned_ref[f, first + k]
                if f == 1 and k == 3:
                    tile = jnp.where(lane < 80, tile, pltpu.roll(turned_ref[0, first + 4], 80, 1))
                outs[d][4 * f + k] = tile


def chunks_kernel(*refs):
    parts, out_ref = refs[:N_LAYER], refs[N_LAYER]
    lane = lane_iota()

    def summed(k):
        total = parts[0][k]
        for part in parts[1:]:
            total = total + part[k]
        return total

    tiles = [summed(k) for k in range(16)]
    stiff = tiles[0:4] + [lanes_left(tiles[7], 80)]
    for t in range(N_TILE):
        a, b = divmod(CHUNK * t, 128)
        inner = lane < 128 - b
        x0 = lanes_left(stiff[a], b)
        x1 = lanes_left(stiff[a + 1], b)
        x2 = lanes_left(stiff[a + 2], b) if a + 2 < 5 else x1
        out_ref[t, 0] = jnp.where(inner, x0, x1)
        tail = jnp.where(inner, x1, x2)
        for f in range(1, 4):
            x = tiles[4 * f : 4 * f + 4]
            x0 = lanes_left(x[a], b)
            x1 = lanes_left(x[a + 1], b) if a + 1 < 4 else x0
            rest = pltpu.roll(tail, NARROW - CHUNK * (f - 1), 1)
            out_ref[t, f] = jnp.where(lane < NARROW, jnp.where(inner, x0, x1), rest)


def put_state(ref, i, u, v):
    for at, x in ((0, u), (3, v)):
        ref[at, i] = x
        ref[at + 1, i] = pltpu.roll(x, 127, 1)
        ref[at + 2, i] = pltpu.roll(x, 1, 1)


def sweep(coef_ref, gu_ref, gv_ref, old, new, n, start):
    def west_side(i):
        return [old[k, i - 1] if i > 0 else pltpu.roll(old[k, n - 1], 1, 0) for k in range(6)]

    west = west_side(start)
    here = [old[k, start] for k in range(6)]
    for step in range(n):
        i = (start + step) % n
        if step and i == 0:
            west = west_side(0)
            here = [old[k, 0] for k in range(6)]
        east = [old[k, i + 1] if i < n - 1 else pltpu.roll(old[k, 0], 7, 0) for k in range(6)]
        half = coef_ref[0, i]
        fresh = []
        for own, other, base, source in ((0, 3, 1, gu_ref), (3, 0, 9, gv_ref)):
            c = [coef_ref[base + k, i] for k in range(8)]
            a = source[i] + half * here[own]
            b = c[0] * here[own + 1] + c[1] * here[own + 2]
            d = c[2] * east[own] + c[3] * west[own]
            e = c[4] * east[other + 1] + c[5] * west[other + 1]
            g = c[6] * east[other + 2] + c[7] * west[other + 2]
            fresh.append((a + b) + (d + (e + g)))
        put_state(new, i, *fresh)
        west, here = here, east


def sweeps(coef_ref, gu_ref, gv_ref, one, two, n):
    def body(_, carry):
        sweep(coef_ref, gu_ref, gv_ref, one, two, n, 0)
        sweep(coef_ref, gu_ref, gv_ref, two, one, n, n // 2)
        return carry

    lax.fori_loop(0, SWEEPS // 2, body, 0)


def up_down():
    lane = lane_iota()
    up_ok = jnp.where(lane < 127, 1.0, 0.0).astype(F32)
    down_ok = jnp.where(lane > 0, 1.0, 0.0).astype(F32)
    return up_ok, down_ok, lambda x: pltpu.roll(x, 127, 1) * up_ok, lambda x: pltpu.roll(x, 1, 1) * down_ok


def east_of(ref, i):
    return ref[i + 1] if i < WB - 1 else pltpu.roll(ref[0], 7, 0)


def west_of(ref, i):
    return ref[i - 1] if i > 0 else pltpu.roll(ref[WB - 1], 1, 0)


def prepare_kernel(x_ref, blk, flat):
    def tile(k):
        return jnp.concatenate(
            [x_ref[t * PACK_ROWS + 8 * k : t * PACK_ROWS + 8 * k + 8, :] for t in range(N_TILE)], 0
        ).T

    for f in range(6):
        flat[f, 0:128, :] = tile(f)
    for k in range(3):
        tail = tile(6 + k)
        flat[2 * k, 128:WIDE, :] = tail[0:56]
        flat[2 * k + 1, 128:WIDE, :] = tail[56:112]
    for f in range(6):
        for i in range(WB):
            blk[f, i] = flat[f, pl.ds(i, 8, stride=WB), :]
    _, _, up, down = up_down()
    u_ref, v_ref = blk.at[0], blk.at[1]
    for i in range(WB):
        u, v = u_ref[i], v_ref[i]
        ux = 0.5 * (up(u) - down(u))
        vx = 0.5 * (up(v) - down(v))
        uy = 0.5 * (east_of(u_ref, i) - west_of(u_ref, i))
        vy = 0.5 * (east_of(v_ref, i) - west_of(v_ref, i))
        shear = uy + vx
        strain = ux * ux + vy * vy + ux * vy + 0.25 * shear * shear + REGULAR
        blk[6, i] = jnp.exp(jnp.log(strain) * (-1.0 / 3.0)) * (0.5 / LAYERS)


def solve_kernel(
    z_ref, blk, out_ref, flat, nu_ref, coef, wide_a, wide_b, tmp, near, near_a, near_b, gu_ref, gv_ref, turned
):
    def tile(k):
        return z_ref[:, k].reshape(128, 128).T

    flat[0, 0:128, :] = tile(0)
    for f in range(1, 4):
        size = min(CHUNK, WIDE - 128 - CHUNK * (f - 1))
        at = 128 + CHUNK * (f - 1)
        flat[0, at : at + size, :] = tile(f)[NARROW : NARROW + size]
    up_ok, down_ok, up, down = up_down()
    for i in range(WB):
        put_state(wide_a, i, blk[0, i], blk[1, i])
        nu_ref[i] = blk[6, i] * flat[0, pl.ds(i, 8, stride=WB), :]
    for i in range(WB):
        nu = nu_ref[i]
        nu_n, nu_s = up(nu), down(nu)
        nu_e, nu_w = east_of(nu_ref, i), west_of(nu_ref, i)
        drag, inside = blk[2, i], blk[3, i]
        n, s, e, w = 0.5 * (nu + nu_n), 0.5 * (nu + nu_s), 0.5 * (nu + nu_e), 0.5 * (nu + nu_w)
        rest = drag + 1.0 - inside
        q_u = 0.5 * inside / (4.0 * (n + s) + (e + w) + rest)
        q_v = 0.5 * inside / ((n + s) + 4.0 * (e + w) + rest)
        coef[0, i] = 0.5 * inside
        coef[1, i] = 4.0 * q_u * n * up_ok
        coef[2, i] = 4.0 * q_u * s * down_ok
        coef[3, i] = q_u * e
        coef[4, i] = q_u * w
        coef[5, i] = q_u * (0.5 * nu_n + 0.25 * nu_e) * up_ok
        coef[6, i] = -q_u * (0.5 * nu_n + 0.25 * nu_w) * up_ok
        coef[7, i] = -q_u * (0.5 * nu_s + 0.25 * nu_e) * down_ok
        coef[8, i] = q_u * (0.5 * nu_s + 0.25 * nu_w) * down_ok
        coef[9, i] = q_v * n * up_ok
        coef[10, i] = q_v * s * down_ok
        coef[11, i] = 4.0 * q_v * e
        coef[12, i] = 4.0 * q_v * w
        coef[13, i] = q_v * (0.5 * nu_e + 0.25 * nu_n) * up_ok
        coef[14, i] = -q_v * (0.5 * nu_w + 0.25 * nu_n) * up_ok
        coef[15, i] = -q_v * (0.5 * nu_e + 0.25 * nu_s) * down_ok
        coef[16, i] = q_v * (0.5 * nu_w + 0.25 * nu_s) * down_ok
        coef[17, i] = q_u * blk[4, i]
        coef[18, i] = q_v * blk[5, i]
        coef[19, i] = q_u
        coef[20, i] = q_v
    for k in range(19):
        j = k if k < 17 else k + 2
        for i in range(WB):
            tmp[k % 4, pl.ds(i, 8, stride=WB), :] = coef[j, i]
        for i in range(NB):
            near[k, i] = tmp[k % 4, pl.ds(SWEEPS + i, 8, stride=NB), :]
    sweeps(coef, coef.at[17], coef.at[18], wide_a, wide_b, WB)
    for i in range(WB):
        flat[0, pl.ds(i, 8, stride=WB), :] = wide_a[0, i]
        flat[1, pl.ds(i, 8, stride=WB), :] = wide_a[3, i]
        flat[2, pl.ds(i, 8, stride=WB), :] = blk[2, i]
    weight = tile(1)[0:NARROW]
    span = slice(SWEEPS, SWEEPS + NARROW)
    tmp[0, 0:NARROW, :] = weight * flat[0, span, :] - tile(2)[0:NARROW]
    tmp[1, 0:NARROW, :] = weight * flat[1, span, :] - tile(3)[0:NARROW]
    for i in range(NB):
        gu_ref[i] = near[17, i] * tmp[0, pl.ds(i, 8, stride=NB), :]
        gv_ref[i] = near[18, i] * tmp[1, pl.ds(i, 8, stride=NB), :]
        for k in range(6):
            near_a[k, i] = jnp.zeros((8, 128), F32)
    sweeps(near, gu_ref, gv_ref, near_a, near_b, NB)
    for i in range(NB):
        tmp[0, pl.ds(i, 8, stride=NB), :] = near_a[0, i]
        tmp[1, pl.ds(i, 8, stride=NB), :] = near_a[3, i]
    own = slice(2 * SWEEPS, 2 * SWEEPS + CHUNK)
    mine = slice(SWEEPS, SWEEPS + CHUNK)
    u, v, drag = flat[0, own, :], flat[1, own, :], flat[2, own, :]
    turned[0:CHUNK, :] = u
    turned[CHUNK : 2 * CHUNK, :] = v
    turned[2 * CHUNK : 3 * CHUNK, :] = -(drag * (u * tmp[0, mine, :] + v * tmp[1, mine, :]))
    turned[3 * CHUNK :, :] = jnp.zeros((128 - 3 * CHUNK, 128), F32)
    tmp[0, 0:128, :] = turned[...].T
    lane = lax.broadcasted_iota(jnp.int32, (N_TILE, 128), 1)
    pieces = [tmp[0, pl.ds(r, N_TILE, stride=8), :] for r in range(8)]
    for k in range(5):
        row = None
        for r in range(8):
            to = 3 * CHUNK * r - 128 * k
            if -3 * CHUNK < to < 128:
                piece = pltpu.roll(pieces[r], to % 128, 1) if to % 128 else pieces[r]
                row = piece if row is None else jnp.where(lane >= to, piece, row)
        for layer in range(N_LAYER):
            out_ref[pl.ds(5 * layer + k, N_TILE, stride=5 * N_LAYER), :] = row


def unpack_kernel(z_ref, vel_ref, grad_ref, rows_ref):
    lane = lane_iota()
    for group in range(N_TILE):
        for r in range(8):
            k, off = divmod(3 * CHUNK * r, 128)
            piece = lanes_left(z_ref[pl.ds(40 * group + k, 8, stride=5), :], off)
            if off + 3 * CHUNK > 128:
                more = lanes_left(z_ref[pl.ds(40 * group + k + 1, 8, stride=5), :], off)
                piece = jnp.where(lane < 128 - off, piece, more)
            rows_ref[pl.ds(64 * group + r, 8, stride=8), :] = piece
    for f in range(3):
        for j in range(TILES):
            tile = None
            for chunk in range(128 * j // CHUNK, (128 * j + 127) // CHUNK + 1):
                layer, t = divmod(chunk, N_TILE)
                to = CHUNK * chunk - 128 * j
                src = 8 * (t * N_LAYER + layer)
                piece = lanes_left(rows_ref[src : src + 8, :], CHUNK * f - to)
                tile = piece if tile is None else jnp.where(lane >= to, piece, tile)
            if f < 2:
                vel_ref[f, :, 128 * j : 128 * j + 128] = tile
            else:
                grad_ref[:, 128 * j : 128 * j + 128] = tile


VMEM = pl.BlockSpec(memory_space=pltpu.VMEM)
SMEM = pl.BlockSpec(memory_space=pltpu.SMEM)


def call(kernel, out_shapes, scratch=(), in_specs=None, flops=1000000, limit=8):
    return pl.pallas_call(
        kernel,
        out_shape=[jax.ShapeDtypeStruct(s, F32) for s in out_shapes],
        in_specs=in_specs,
        out_specs=[VMEM] * len(out_shapes),
        scratch_shapes=list(scratch),
        cost_estimate=pl.CostEstimate(flops=flops, bytes_accessed=1000000, transcendentals=0),
        compiler_params=pltpu.CompilerParams(vmem_limit_bytes=limit << 20),
    )


def exchange(x, axis):
    return lax.all_to_all(x, axis, split_axis=0, concat_axis=0, tiled=True)


def to_layers(blocks):
    out = [blocks[0]]
    for d in range(1, N_LAYER):
        out.append(lax.ppermute(blocks[d], "layer", [(i, (i + d) % N_LAYER) for i in range(N_LAYER)]))
    return out


def on_device(
    velocity_guess, hardness, thickness, friction, grounded, ice_mask, driving,
    obs_cell, obs_east, obs_north, obs_weight, obs_count,
):
    slots = (N_TILE, BLOCK)
    me = lax.axis_index("layer").astype(jnp.int32).reshape(1)
    (packed,) = call(pack_kernel, [(N_TILE * PACK_ROWS, 128)], in_specs=[SMEM] * 2 + [VMEM] * 9, limit=58)(
        me, obs_count.reshape(1, N_TILE), obs_cell.reshape(slots), obs_east.reshape(slots),
        obs_north.reshape(slots), obs_weight.reshape(slots),
        velocity_guess, friction, grounded, ice_mask, driving,
    )
    arrived = exchange(packed.reshape(N_TILE, PACK_ROWS, 128), "tile").reshape(N_TILE * PACK_ROWS, 128)
    (stiff,) = call(stiffness_kernel, [(8, COLS)], in_specs=[VMEM] * 2)(hardness, thickness)
    parts = call(
        scatter_kernel,
        [(16, 8, 128)] * N_LAYER,
        scratch=[
            pltpu.VMEM((3 * PIECES * 96, DEPTH), jnp.bfloat16),
            pltpu.VMEM((256, DEPTH), jnp.bfloat16),
            pltpu.VMEM((3 * PIECES * 96, 256), F32),
            pltpu.VMEM((4, TILES + 2, 8, 128), F32),
        ],
        in_specs=[SMEM] + [VMEM] * 2,
        flops=3600000000,
        limit=16,
    )(me, arrived, stiff)
    parts = to_layers(parts)
    (blocks,) = call(
        prepare_kernel, [(7, WB, 8, 128)], scratch=[pltpu.VMEM((6, WIDE, 128), F32)], in_specs=[VMEM]
    )(arrived)
    (chunks,) = call(chunks_kernel, [(N_TILE, 4, 8, 128)], in_specs=[VMEM] * N_LAYER)(*parts)
    chunks = exchange(chunks, "tile")
    (shares,) = call(
        solve_kernel,
        [(N_TILE * N_LAYER * 5, 128)],
        scratch=[
            pltpu.VMEM((3, WIDE, 128), F32),
            pltpu.VMEM((WB, 8, 128), F32),
            pltpu.VMEM((21, WB, 8, 128), F32),
            pltpu.VMEM((6, WB, 8, 128), F32),
            pltpu.VMEM((6, WB, 8, 128), F32),
            pltpu.VMEM((4, WIDE, 128), F32),
            pltpu.VMEM((19, NB, 8, 128), F32),
            pltpu.VMEM((6, NB, 8, 128), F32),
            pltpu.VMEM((6, NB, 8, 128), F32),
            pltpu.VMEM((NB, 8, 128), F32),
            pltpu.VMEM((NB, 8, 128), F32),
            pltpu.VMEM((128, 128), F32),
        ],
        in_specs=[VMEM] * 2,
        flops=3600000000,
        limit=16,
    )(chunks, blocks)
    shares = exchange(shares.reshape(N_TILE * N_LAYER * 5 * 128), ("tile", "layer"))
    velocity, gradient = call(
        unpack_kernel,
        [(2, 8, COLS), (8, COLS)],
        scratch=[pltpu.VMEM((N_TILE * N_LAYER * 8, 128), F32)],
        in_specs=[VMEM],
    )(shares.reshape(N_TILE * N_LAYER * 5, 128))
    return velocity, gradient


def solution(mesh):
    return jax.shard_map(
        on_device,
        mesh=mesh,
        in_specs=(
            P(None, "tile", None),
            P("layer", "tile", None),
            P("tile", None),
            P("tile", None),
            P("tile", None),
            P("tile", None),
            P(None, "tile", None),
            P("tile", "layer", None, None),
            P("tile", "layer", None, None),
            P("tile", "layer", None, None),
            P("tile", "layer", None, None),
            P("tile", "layer", None),
        ),
        out_specs=(P(None, "tile", None), P("tile", None)),
        check_vma=False,
    )
```

```python
import jax
import jax.numpy as jnp
from jax import lax
from jax.experimental import pallas as pl
from jax.experimental.pallas import tpu as pltpu
from jax.sharding import PartitionSpec as P

SWEEPS = 40
LAYERS = 32
REGULAR = 0.01

ROWS = 8
COLS = 3072
TILES = COLS // 128
N_TILE = 16
N_LAYER = 8
BLOCK = 512
CHUNK = 24
WIDE = CHUNK + 4 * SWEEPS
NARROW = CHUNK + 2 * SWEEPS
WB = WIDE // 8
NB = NARROW // 8
SHARE = COLS // N_LAYER
F32 = jnp.float32
PACK_ROWS = 8 * 11
PIECES = 3
UNROLL = 20
DEPTH = 2048
OBS_ROWS = PACK_ROWS
OBS_AT = 72


def lane_iota():
    return lax.broadcasted_iota(jnp.int32, (8, 128), 1)


def lanes_left(x, by):
    by = by % 128
    return pltpu.roll(x, 128 - by, 1) if by else x


def pack_kernel(
    me_ref, count_ref, cell_ref, east_ref, north_ref, weight_ref,
    guess_ref, fric_ref, ground_ref, ice_ref, drive_ref, out_ref,
):
    row = lax.broadcasted_iota(jnp.int32, (N_TILE, BLOCK), 0)
    slot = lax.broadcasted_iota(jnp.int32, (N_TILE, BLOCK), 1)
    count = jnp.zeros((N_TILE, BLOCK), jnp.int32)
    for d in range(N_TILE):
        count = jnp.where(row == d, count_ref[0, d], count)
    weight = jnp.where(slot < count, weight_ref[...], 0.0)
    cell = cell_ref[...]
    high = cell >> 8
    strip_row = ((cell >> 10) * 11) >> 5
    place = ((high - strip_row * (COLS // 256)) * ROWS + strip_row) * 256 + (cell & 255)
    for f, x in enumerate((place.astype(F32), weight, weight * east_ref[...], weight * north_ref[...])):
        for k in range(4):
            for half in range(2):
                at = pl.ds(8 * half * PACK_ROWS + 8 * 9 + 4 * f + k, 8, stride=PACK_ROWS)
                out_ref[at, :] = x[8 * half : 8 * half + 8, 128 * k : 128 * k + 128]

    first = 3 * me_ref[0] - 1
    lane = lane_iota()
    fields = [[] for _ in range(6)]
    for k in range(5):
        g = first + k
        keep = jnp.where(jnp.logical_and(g >= 0, g < TILES), 1.0, 0.0).astype(F32)
        at = pl.ds(pl.multiple_of(jnp.clip(g, 0, TILES - 1) * 128, 128), 128)
        fields[0].append(guess_ref[0, :, at] * keep)
        fields[1].append(guess_ref[1, :, at] * keep)
        fields[2].append(fric_ref[:, at] * ground_ref[:, at].astype(F32) * keep)
        fields[3].append(ice_ref[:, at].astype(F32) * keep)
        fields[4].append(drive_ref[0, :, at] * keep)
        fields[5].append(drive_ref[1, :, at] * keep)
    for t in range(N_TILE):
        a, b = divmod(48 + CHUNK * t, 128)
        inner = lane < 128 - b
        tails = []
        for f in range(6):
            x0 = lanes_left(fields[f][a], b)
            x1 = lanes_left(fields[f][a + 1], b)
            x2 = lanes_left(fields[f][a + 2], b) if a + 2 < 5 else x1
            out_ref[t * PACK_ROWS + 8 * f : t * PACK_ROWS + 8 * f + 8, :] = jnp.where(inner, x0, x1)
            tails.append(jnp.where(inner, x1, x2))
        for k in range(3):
            at = t * PACK_ROWS + 8 * (6 + k)
            out_ref[at : at + 8, :] = jnp.where(lane < 56, tails[2 * k], pltpu.roll(tails[2 * k + 1], 56, 1))


def stiffness_kernel(hard_ref, thick_ref, out_ref):
    for g in range(TILES):
        at = slice(128 * g, 128 * g + 128)
        part = (hard_ref[0, :, at] + hard_ref[1, :, at]) + (hard_ref[2, :, at] + hard_ref[3, :, at])
        out_ref[:, at] = thick_ref[:, at] * part


def scatter_kernel(me_ref, obs_ref, stiff_ref, *refs):
    outs, (lhs_ref, rhs_ref, acc_ref, turned_ref) = refs[:N_LAYER], refs[N_LAYER:]
    acc_ref[...] = jnp.zeros_like(acc_ref)
    step16 = lax.broadcasted_iota(jnp.int32, (16, 128), 0).astype(F32).astype(jnp.bfloat16)
    zero16 = jnp.zeros((16, 128), jnp.bfloat16)
    one16 = jnp.ones((16, 128), jnp.bfloat16)

    def rows(x):
        return jnp.broadcast_to(x, (16, 128)).astype(jnp.bfloat16)

    def body(step, carry):
        for q in range(DEPTH // 128):
            lanes = slice(128 * q, 128 * q + 128)
            base = (step * (DEPTH // BLOCK) + q // 4) * OBS_ROWS + OBS_AT + q % 4
            place = obs_ref[pl.ds(base, 1), :].astype(jnp.int32)
            high = rows((place >> 8).astype(F32))
            low = rows((place & 255).astype(F32))
            pieces = []
            for f in range(3):
                value = obs_ref[pl.ds(base + 4 * (f + 1), 1), :]
                for k in range(PIECES):
                    piece = value.astype(jnp.bfloat16).astype(F32)
                    pieces.append(rows(piece))
                    if k < PIECES - 1:
                        value = value - piece
            for b in range(16):
                rhs_ref[16 * b : 16 * b + 16, lanes] = jnp.where(low == step16 + 16.0 * b, one16, zero16)
            for b in range(6):
                hit = high == step16 + 16.0 * b
                for k in range(3 * PIECES):
                    lhs_ref[k * 96 + 16 * b : k * 96 + 16 * b + 16, lanes] = jnp.where(hit, pieces[k], zero16)
        acc_ref[...] += lax.dot_general(
            lhs_ref[...], rhs_ref[...], (((1,), (1,)), ((), ())), preferred_element_type=F32
        )
        return carry

    lax.fori_loop(0, N_TILE * BLOCK // DEPTH, body, 0)
    lane = lane_iota()
    zero = jnp.zeros((8, 128), F32)

    def turn(f, tiles, shift):
        turned = [zero] + [lanes_left(x, shift) for x in tiles] + [zero, zero]
        for g in range(TILES + 2):
            turned_ref[f, g] = jnp.where(lane < 128 - shift, turned[g], turned[g + 1])

    turn(0, [stiff_ref[:, 128 * g : 128 * g + 128] for g in range(TILES)], 48)
    for f in range(3):
        total = acc_ref[PIECES * f * 96 : PIECES * f * 96 + 96, :]
        for k in range(1, PIECES):
            total = total + acc_ref[(PIECES * f + k) * 96 : (PIECES * f + k + 1) * 96, :]
        tiles = [total[8 * (g // 2) : 8 * (g // 2) + 8, 128 * (g % 2) : 128 * (g % 2) + 128] for g in range(TILES)]
        turn(f + 1, tiles, 88)
    for d in range(N_LAYER):
        first = 3 * ((me_ref[0] + d) & (N_LAYER - 1))
        for f in range(4):
            for k in range(4):
                tile = turned_ref[f, first + k]
                if f == 1 and k == 3:
                    tile = jnp.where(lane < 80, tile, pltpu.roll(turned_ref[0, first + 4], 80, 1))
                outs[d][4 * f + k] = tile


def chunks_kernel(*refs):
    parts, out_ref = refs[:N_LAYER], refs[N_LAYER]
    lane = lane_iota()

    def summed(k):
        total = parts[0][k]
        for part in parts[1:]:
            total = total + part[k]
        return total

    tiles = [summed(k) for k in range(16)]
    stiff = tiles[0:4] + [lanes_left(tiles[7], 80)]
    for t in range(N_TILE):
        a, b = divmod(CHUNK * t, 128)
        inner = lane < 128 - b
        x0 = lanes_left(stiff[a], b)
        x1 = lanes_left(stiff[a + 1], b)
        x2 = lanes_left(stiff[a + 2], b) if a + 2 < 5 else x1
        out_ref[t, 0] = jnp.where(inner, x0, x1)
        tail = jnp.where(inner, x1, x2)
        for f in range(1, 4):
            x = tiles[4 * f : 4 * f + 4]
            x0 = lanes_left(x[a], b)
            x1 = lanes_left(x[a + 1], b) if a + 1 < 4 else x0
            rest = pltpu.roll(tail, NARROW - CHUNK * (f - 1), 1)
            out_ref[t, f] = jnp.where(lane < NARROW, jnp.where(inner, x0, x1), rest)


def put_state(ref, i, u, v):
    for at, x in ((0, u), (3, v)):
        ref[at, i] = x
        ref[at + 1, i] = pltpu.roll(x, 127, 1)
        ref[at + 2, i] = pltpu.roll(x, 1, 1)


def sweep(coef_ref, gu_ref, gv_ref, old, new, n, start):
    def west_side(i):
        return [old[k, i - 1] if i > 0 else pltpu.roll(old[k, n - 1], 1, 0) for k in range(6)]

    west = west_side(start)
    here = [old[k, start] for k in range(6)]
    for step in range(n):
        i = (start + step) % n
        if step and i == 0:
            west = west_side(0)
            here = [old[k, 0] for k in range(6)]
        east = [old[k, i + 1] if i < n - 1 else pltpu.roll(old[k, 0], 7, 0) for k in range(6)]
        half = coef_ref[0, i]
        fresh = []
        for own, other, base, source in ((0, 3, 1, gu_ref), (3, 0, 9, gv_ref)):
            c = [coef_ref[base + k, i] for k in range(8)]
            a = source[i] + half * here[own]
            b = c[0] * here[own + 1] + c[1] * here[own + 2]
            d = c[2] * east[own] + c[3] * west[own]
            e = c[4] * east[other + 1] + c[5] * west[other + 1]
            g = c[6] * east[other + 2] + c[7] * west[other + 2]
            fresh.append((a + b) + (d + (e + g)))
        put_state(new, i, *fresh)
        west, here = here, east


def sweeps(coef_ref, gu_ref, gv_ref, one, two, n):
    def body(_, carry):
        for k in range(UNROLL):
            old, new = (one, two) if k % 2 == 0 else (two, one)
            sweep(coef_ref, gu_ref, gv_ref, old, new, n, (n // 4 * k) % n)
        return carry

    lax.fori_loop(0, SWEEPS // UNROLL, body, 0)


def up_down():
    lane = lane_iota()
    up_ok = jnp.where(lane < 127, 1.0, 0.0).astype(F32)
    down_ok = jnp.where(lane > 0, 1.0, 0.0).astype(F32)
    return up_ok, down_ok, lambda x: pltpu.roll(x, 127, 1) * up_ok, lambda x: pltpu.roll(x, 1, 1) * down_ok


def east_of(ref, i):
    return ref[i + 1] if i < WB - 1 else pltpu.roll(ref[0], 7, 0)


def west_of(ref, i):
    return ref[i - 1] if i > 0 else pltpu.roll(ref[WB - 1], 1, 0)


def prepare_kernel(x_ref, blk, flat):
    def tile(k):
        return jnp.concatenate(
            [x_ref[t * PACK_ROWS + 8 * k : t * PACK_ROWS + 8 * k + 8, :] for t in range(N_TILE)], 0
        ).T

    for f in range(6):
        flat[f, 0:128, :] = tile(f)
    for k in range(3):
        tail = tile(6 + k)
        flat[2 * k, 128:WIDE, :] = tail[0:56]
        flat[2 * k + 1, 128:WIDE, :] = tail[56:112]
    for f in range(6):
        for i in range(WB):
            blk[f, i] = flat[f, pl.ds(i, 8, stride=WB), :]
    _, _, up, down = up_down()
    u_ref, v_ref = blk.at[0], blk.at[1]
    for i in range(WB):
        u, v = u_ref[i], v_ref[i]
        ux = 0.5 * (up(u) - down(u))
        vx = 0.5 * (up(v) - down(v))
        uy = 0.5 * (east_of(u_ref, i) - west_of(u_ref, i))
        vy = 0.5 * (east_of(v_ref, i) - west_of(v_ref, i))
        shear = uy + vx
        strain = ux * ux + vy * vy + ux * vy + 0.25 * shear * shear + REGULAR
        blk[6, i] = jnp.exp(jnp.log(strain) * (-1.0 / 3.0)) * (0.5 / LAYERS)


def solve_kernel(
    z_ref, blk, out_ref, flat, nu_ref, coef, wide_a, wide_b, tmp, near, near_a, near_b, gu_ref, gv_ref, turned
):
    def tile(k):
        return z_ref[:, k].reshape(128, 128).T

    flat[0, 0:128, :] = tile(0)
    for f in range(1, 4):
        size = min(CHUNK, WIDE - 128 - CHUNK * (f - 1))
        at = 128 + CHUNK * (f - 1)
        flat[0, at : at + size, :] = tile(f)[NARROW : NARROW + size]
    up_ok, down_ok, up, down = up_down()
    for i in range(WB):
        put_state(wide_a, i, blk[0, i], blk[1, i])
        nu_ref[i] = blk[6, i] * flat[0, pl.ds(i, 8, stride=WB), :]
    for i in range(WB):
        nu = nu_ref[i]
        nu_n, nu_s = up(nu), down(nu)
        nu_e, nu_w = east_of(nu_ref, i), west_of(nu_ref, i)
        drag, inside = blk[2, i], blk[3, i]
        n, s, e, w = 0.5 * (nu + nu_n), 0.5 * (nu + nu_s), 0.5 * (nu + nu_e), 0.5 * (nu + nu_w)
        rest = drag + 1.0 - inside
        q_u = 0.5 * inside / (4.0 * (n + s) + (e + w) + rest)
        q_v = 0.5 * inside / ((n + s) + 4.0 * (e + w) + rest)
        coef[0, i] = 0.5 * inside
        coef[1, i] = 4.0 * q_u * n * up_ok
        coef[2, i] = 4.0 * q_u * s * down_ok
        coef[3, i] = q_u * e
        coef[4, i] = q_u * w
        coef[5, i] = q_u * (0.5 * nu_n + 0.25 * nu_e) * up_ok
        coef[6, i] = -q_u * (0.5 * nu_n + 0.25 * nu_w) * up_ok
        coef[7, i] = -q_u * (0.5 * nu_s + 0.25 * nu_e) * down_ok
        coef[8, i] = q_u * (0.5 * nu_s + 0.25 * nu_w) * down_ok
        coef[9, i] = q_v * n * up_ok
        coef[10, i] = q_v * s * down_ok
        coef[11, i] = 4.0 * q_v * e
        coef[12, i] = 4.0 * q_v * w
        coef[13, i] = q_v * (0.5 * nu_e + 0.25 * nu_n) * up_ok
        coef[14, i] = -q_v * (0.5 * nu_w + 0.25 * nu_n) * up_ok
        coef[15, i] = -q_v * (0.5 * nu_e + 0.25 * nu_s) * down_ok
        coef[16, i] = q_v * (0.5 * nu_w + 0.25 * nu_s) * down_ok
        coef[17, i] = q_u * blk[4, i]
        coef[18, i] = q_v * blk[5, i]
        coef[19, i] = q_u
        coef[20, i] = q_v
    for k in range(19):
        j = k if k < 17 else k + 2
        for i in range(WB):
            tmp[k % 4, pl.ds(i, 8, stride=WB), :] = coef[j, i]
        for i in range(NB):
            near[k, i] = tmp[k % 4, pl.ds(SWEEPS + i, 8, stride=NB), :]
    sweeps(coef, coef.at[17], coef.at[18], wide_a, wide_b, WB)
    for i in range(WB):
        flat[0, pl.ds(i, 8, stride=WB), :] = wide_a[0, i]
        flat[1, pl.ds(i, 8, stride=WB), :] = wide_a[3, i]
        flat[2, pl.ds(i, 8, stride=WB), :] = blk[2, i]
    weight = tile(1)[0:NARROW]
    span = slice(SWEEPS, SWEEPS + NARROW)
    tmp[0, 0:NARROW, :] = weight * flat[0, span, :] - tile(2)[0:NARROW]
    tmp[1, 0:NARROW, :] = weight * flat[1, span, :] - tile(3)[0:NARROW]
    for i in range(NB):
        gu_ref[i] = near[17, i] * tmp[0, pl.ds(i, 8, stride=NB), :]
        gv_ref[i] = near[18, i] * tmp[1, pl.ds(i, 8, stride=NB), :]
        for k in range(6):
            near_a[k, i] = jnp.zeros((8, 128), F32)
    sweeps(near, gu_ref, gv_ref, near_a, near_b, NB)
    for i in range(NB):
        tmp[0, pl.ds(i, 8, stride=NB), :] = near_a[0, i]
        tmp[1, pl.ds(i, 8, stride=NB), :] = near_a[3, i]
    own = slice(2 * SWEEPS, 2 * SWEEPS + CHUNK)
    mine = slice(SWEEPS, SWEEPS + CHUNK)
    u, v, drag = flat[0, own, :], flat[1, own, :], flat[2, own, :]
    turned[0:CHUNK, :] = u
    turned[CHUNK : 2 * CHUNK, :] = v
    turned[2 * CHUNK : 3 * CHUNK, :] = -(drag * (u * tmp[0, mine, :] + v * tmp[1, mine, :]))
    turned[3 * CHUNK :, :] = jnp.zeros((128 - 3 * CHUNK, 128), F32)
    tmp[0, 0:128, :] = turned[...].T
    lane = lax.broadcasted_iota(jnp.int32, (N_TILE, 128), 1)
    pieces = [tmp[0, pl.ds(r, N_TILE, stride=8), :] for r in range(8)]
    for k in range(5):
        row = None
        for r in range(8):
            to = 3 * CHUNK * r - 128 * k
            if -3 * CHUNK < to < 128:
                piece = pltpu.roll(pieces[r], to % 128, 1) if to % 128 else pieces[r]
                row = piece if row is None else jnp.where(lane >= to, piece, row)
        for layer in range(N_LAYER):
            out_ref[pl.ds(5 * layer + k, N_TILE, stride=5 * N_LAYER), :] = row


def unpack_kernel(z_ref, vel_ref, grad_ref, rows_ref):
    lane = lane_iota()
    for group in range(N_TILE):
        for r in range(8):
            k, off = divmod(3 * CHUNK * r, 128)
            piece = lanes_left(z_ref[pl.ds(40 * group + k, 8, stride=5), :], off)
            if off + 3 * CHUNK > 128:
                more = lanes_left(z_ref[pl.ds(40 * group + k + 1, 8, stride=5), :], off)
                piece = jnp.where(lane < 128 - off, piece, more)
            rows_ref[pl.ds(64 * group + r, 8, stride=8), :] = piece
    for f in range(3):
        for j in range(TILES):
            tile = None
            for chunk in range(128 * j // CHUNK, (128 * j + 127) // CHUNK + 1):
                layer, t = divmod(chunk, N_TILE)
                to = CHUNK * chunk - 128 * j
                src = 8 * (t * N_LAYER + layer)
                piece = lanes_left(rows_ref[src : src + 8, :], CHUNK * f - to)
                tile = piece if tile is None else jnp.where(lane >= to, piece, tile)
            if f < 2:
                vel_ref[f, :, 128 * j : 128 * j + 128] = tile
            else:
                grad_ref[:, 128 * j : 128 * j + 128] = tile


VMEM = pl.BlockSpec(memory_space=pltpu.VMEM)
SMEM = pl.BlockSpec(memory_space=pltpu.SMEM)


def call(kernel, out_shapes, scratch=(), in_specs=None, flops=1000000, limit=8):
    return pl.pallas_call(
        kernel,
        out_shape=[jax.ShapeDtypeStruct(s, F32) for s in out_shapes],
        in_specs=in_specs,
        out_specs=[VMEM] * len(out_shapes),
        scratch_shapes=list(scratch),
        cost_estimate=pl.CostEstimate(flops=flops, bytes_accessed=1000000, transcendentals=0),
        compiler_params=pltpu.CompilerParams(vmem_limit_bytes=limit << 20),
    )


def exchange(x, axis):
    return lax.all_to_all(x, axis, split_axis=0, concat_axis=0, tiled=True)


def to_layers(blocks):
    out = [blocks[0]]
    for d in range(1, N_LAYER):
        out.append(lax.ppermute(blocks[d], "layer", [(i, (i + d) % N_LAYER) for i in range(N_LAYER)]))
    return out


def on_device(
    velocity_guess, hardness, thickness, friction, grounded, ice_mask, driving,
    obs_cell, obs_east, obs_north, obs_weight, obs_count,
):
    slots = (N_TILE, BLOCK)
    me = lax.axis_index("layer").astype(jnp.int32).reshape(1)
    (packed,) = call(pack_kernel, [(N_TILE * PACK_ROWS, 128)], in_specs=[SMEM] * 2 + [VMEM] * 9, limit=58)(
        me, obs_count.reshape(1, N_TILE), obs_cell.reshape(slots), obs_east.reshape(slots),
        obs_north.reshape(slots), obs_weight.reshape(slots),
        velocity_guess, friction, grounded, ice_mask, driving,
    )
    arrived = exchange(packed.reshape(N_TILE, PACK_ROWS, 128), "tile").reshape(N_TILE * PACK_ROWS, 128)
    (stiff,) = call(stiffness_kernel, [(8, COLS)], in_specs=[VMEM] * 2)(hardness, thickness)
    parts = call(
        scatter_kernel,
        [(16, 8, 128)] * N_LAYER,
        scratch=[
            pltpu.VMEM((3 * PIECES * 96, DEPTH), jnp.bfloat16),
            pltpu.VMEM((256, DEPTH), jnp.bfloat16),
            pltpu.VMEM((3 * PIECES * 96, 256), F32),
            pltpu.VMEM((4, TILES + 2, 8, 128), F32),
        ],
        in_specs=[SMEM] + [VMEM] * 2,
        flops=3600000000,
        limit=16,
    )(me, arrived, stiff)
    parts = to_layers(parts)
    (blocks,) = call(
        prepare_kernel, [(7, WB, 8, 128)], scratch=[pltpu.VMEM((6, WIDE, 128), F32)], in_specs=[VMEM]
    )(arrived)
    (chunks,) = call(chunks_kernel, [(N_TILE, 4, 8, 128)], in_specs=[VMEM] * N_LAYER)(*parts)
    chunks = exchange(chunks, "tile")
    (shares,) = call(
        solve_kernel,
        [(N_TILE * N_LAYER * 5, 128)],
        scratch=[
            pltpu.VMEM((3, WIDE, 128), F32),
            pltpu.VMEM((WB, 8, 128), F32),
            pltpu.VMEM((21, WB, 8, 128), F32),
            pltpu.VMEM((6, WB, 8, 128), F32),
            pltpu.VMEM((6, WB, 8, 128), F32),
            pltpu.VMEM((4, WIDE, 128), F32),
            pltpu.VMEM((19, NB, 8, 128), F32),
            pltpu.VMEM((6, NB, 8, 128), F32),
            pltpu.VMEM((6, NB, 8, 128), F32),
            pltpu.VMEM((NB, 8, 128), F32),
            pltpu.VMEM((NB, 8, 128), F32),
            pltpu.VMEM((128, 128), F32),
        ],
        in_specs=[VMEM] * 2,
        flops=3600000000,
        limit=16,
    )(chunks, blocks)
    shares = exchange(shares.reshape(N_TILE * N_LAYER * 5 * 128), ("tile", "layer"))
    velocity, gradient = call(
        unpack_kernel,
        [(2, 8, COLS), (8, COLS)],
        scratch=[pltpu.VMEM((N_TILE * N_LAYER * 8, 128), F32)],
        in_specs=[VMEM],
    )(shares.reshape(N_TILE * N_LAYER * 5, 128))
    return velocity, gradient


def solution(mesh):
    return jax.shard_map(
        on_device,
        mesh=mesh,
        in_specs=(
            P(None, "tile", None),
            P("layer", "tile", None),
            P("tile", None),
            P("tile", None),
            P("tile", None),
            P("tile", None),
            P(None, "tile", None),
            P("tile", "layer", None, None),
            P("tile", "layer", None, None),
            P("tile", "layer", None, None),
            P("tile", "layer", None, None),
            P("tile", "layer", None),
        ),
        out_specs=(P(None, "tile", None), P("tile", None)),
        check_vma=False,
    )
```

```python
import jax
import jax.numpy as jnp
from jax import lax
from jax.experimental import pallas as pl
from jax.experimental.pallas import tpu as pltpu
from jax.sharding import PartitionSpec as P

SWEEPS = 40
LAYERS = 32
REGULAR = 0.01

ROWS = 8
COLS = 3072
TILES = COLS // 128
N_TILE = 16
N_LAYER = 8
N_CHIP = N_LAYER // 2
BLOCK = 512
CHUNK = 24
WIDE = CHUNK + 4 * SWEEPS
NARROW = CHUNK + 2 * SWEEPS
WB = WIDE // 8
NB = NARROW // 8
SHARE = COLS // N_LAYER
F32 = jnp.float32
PACK_ROWS = 8 * 11
PIECES = 3
UNROLL = 20
DEPTH = 2048
OBS_ROWS = PACK_ROWS
OBS_AT = 72


def lane_iota():
    return lax.broadcasted_iota(jnp.int32, (8, 128), 1)


def lanes_left(x, by):
    by = by % 128
    return pltpu.roll(x, 128 - by, 1) if by else x


def pack_kernel(
    me_ref, count_ref, cell_ref, east_ref, north_ref, weight_ref,
    guess_ref, fric_ref, ground_ref, ice_ref, drive_ref, out_ref,
):
    row = lax.broadcasted_iota(jnp.int32, (N_TILE, BLOCK), 0)
    slot = lax.broadcasted_iota(jnp.int32, (N_TILE, BLOCK), 1)
    count = jnp.zeros((N_TILE, BLOCK), jnp.int32)
    for d in range(N_TILE):
        count = jnp.where(row == d, count_ref[0, d], count)
    weight = jnp.where(slot < count, weight_ref[...], 0.0)
    cell = cell_ref[...]
    high = cell >> 8
    strip_row = ((cell >> 10) * 11) >> 5
    place = ((high - strip_row * (COLS // 256)) * ROWS + strip_row) * 256 + (cell & 255)
    for f, x in enumerate((place.astype(F32), weight, weight * east_ref[...], weight * north_ref[...])):
        for k in range(4):
            for half in range(2):
                at = pl.ds(8 * half * PACK_ROWS + 8 * 9 + 4 * f + k, 8, stride=PACK_ROWS)
                out_ref[at, :] = x[8 * half : 8 * half + 8, 128 * k : 128 * k + 128]

    first = 3 * me_ref[0] - 1
    lane = lane_iota()
    fields = [[] for _ in range(6)]
    for k in range(5):
        g = first + k
        keep = jnp.where(jnp.logical_and(g >= 0, g < TILES), 1.0, 0.0).astype(F32)
        at = pl.ds(pl.multiple_of(jnp.clip(g, 0, TILES - 1) * 128, 128), 128)
        fields[0].append(guess_ref[0, :, at] * keep)
        fields[1].append(guess_ref[1, :, at] * keep)
        fields[2].append(fric_ref[:, at] * ground_ref[:, at].astype(F32) * keep)
        fields[3].append(ice_ref[:, at].astype(F32) * keep)
        fields[4].append(drive_ref[0, :, at] * keep)
        fields[5].append(drive_ref[1, :, at] * keep)
    for t in range(N_TILE):
        a, b = divmod(48 + CHUNK * t, 128)
        inner = lane < 128 - b
        tails = []
        for f in range(6):
            x0 = lanes_left(fields[f][a], b)
            x1 = lanes_left(fields[f][a + 1], b)
            x2 = lanes_left(fields[f][a + 2], b) if a + 2 < 5 else x1
            out_ref[t * PACK_ROWS + 8 * f : t * PACK_ROWS + 8 * f + 8, :] = jnp.where(inner, x0, x1)
            tails.append(jnp.where(inner, x1, x2))
        for k in range(3):
            at = t * PACK_ROWS + 8 * (6 + k)
            out_ref[at : at + 8, :] = jnp.where(lane < 56, tails[2 * k], pltpu.roll(tails[2 * k + 1], 56, 1))


def stiffness_kernel(hard_ref, thick_ref, out_ref):
    for g in range(TILES):
        at = slice(128 * g, 128 * g + 128)
        part = (hard_ref[0, :, at] + hard_ref[1, :, at]) + (hard_ref[2, :, at] + hard_ref[3, :, at])
        out_ref[:, at] = thick_ref[:, at] * part


def scatter_kernel(me_ref, obs_ref, stiff_ref, *refs):
    outs, (lhs_ref, rhs_ref, acc_ref, turned_ref) = refs[:2], refs[2:]
    acc_ref[...] = jnp.zeros_like(acc_ref)
    step16 = lax.broadcasted_iota(jnp.int32, (16, 128), 0).astype(F32).astype(jnp.bfloat16)
    zero16 = jnp.zeros((16, 128), jnp.bfloat16)
    one16 = jnp.ones((16, 128), jnp.bfloat16)

    def rows(x):
        return jnp.broadcast_to(x, (16, 128)).astype(jnp.bfloat16)

    def body(step, carry):
        for q in range(DEPTH // 128):
            lanes = slice(128 * q, 128 * q + 128)
            base = (step * (DEPTH // BLOCK) + q // 4) * OBS_ROWS + OBS_AT + q % 4
            place = obs_ref[pl.ds(base, 1), :].astype(jnp.int32)
            high = rows((place >> 8).astype(F32))
            low = rows((place & 255).astype(F32))
            pieces = []
            for f in range(3):
                value = obs_ref[pl.ds(base + 4 * (f + 1), 1), :]
                for k in range(PIECES):
                    piece = value.astype(jnp.bfloat16).astype(F32)
                    pieces.append(rows(piece))
                    if k < PIECES - 1:
                        value = value - piece
            for b in range(16):
                rhs_ref[16 * b : 16 * b + 16, lanes] = jnp.where(low == step16 + 16.0 * b, one16, zero16)
            for b in range(6):
                hit = high == step16 + 16.0 * b
                for k in range(3 * PIECES):
                    lhs_ref[k * 96 + 16 * b : k * 96 + 16 * b + 16, lanes] = jnp.where(hit, pieces[k], zero16)
        acc_ref[...] += lax.dot_general(
            lhs_ref[...], rhs_ref[...], (((1,), (1,)), ((), ())), preferred_element_type=F32
        )
        return carry

    lax.fori_loop(0, N_TILE * BLOCK // DEPTH, body, 0)
    lane = lane_iota()
    zero = jnp.zeros((8, 128), F32)

    def turn(f, tiles, shift):
        turned = [zero] + [lanes_left(x, shift) for x in tiles] + [zero, zero]
        for g in range(TILES + 2):
            turned_ref[f, g] = jnp.where(lane < 128 - shift, turned[g], turned[g + 1])

    turn(0, [stiff_ref[:, 128 * g : 128 * g + 128] for g in range(TILES)], 48)
    for f in range(3):
        total = acc_ref[PIECES * f * 96 : PIECES * f * 96 + 96, :]
        for k in range(1, PIECES):
            total = total + acc_ref[(PIECES * f + k) * 96 : (PIECES * f + k + 1) * 96, :]
        tiles = [total[8 * (g // 2) : 8 * (g // 2) + 8, 128 * (g % 2) : 128 * (g % 2) + 128] for g in range(TILES)]
        turn(f + 1, tiles, 88)
    chip, core = me_ref[0] >> 1, me_ref[0] & 1
    for side in range(2):
        for d in range(N_CHIP):
            first = 3 * (2 * ((chip + d) & (N_CHIP - 1)) + (core ^ side))
            for f in range(4):
                for k in range(4):
                    tile = turned_ref[f, first + k]
                    if f == 1 and k == 3:
                        tile = jnp.where(lane < 80, tile, pltpu.roll(turned_ref[0, first + 4], 80, 1))
                    outs[side][d, 4 * f + k] = tile


def add_kernel(a_ref, b_ref, *outs):
    for d in range(N_CHIP):
        outs[d][...] = a_ref[d] + b_ref[d]


def chunks_kernel(*refs):
    parts, out_ref = refs[:N_CHIP], refs[N_CHIP]
    lane = lane_iota()

    def summed(k):
        total = parts[0][k]
        for part in parts[1:]:
            total = total + part[k]
        return total

    tiles = [summed(k) for k in range(16)]
    stiff = tiles[0:4] + [lanes_left(tiles[7], 80)]
    for t in range(N_TILE):
        a, b = divmod(CHUNK * t, 128)
        inner = lane < 128 - b
        x0 = lanes_left(stiff[a], b)
        x1 = lanes_left(stiff[a + 1], b)
        x2 = lanes_left(stiff[a + 2], b) if a + 2 < 5 else x1
        out_ref[t, 0] = jnp.where(inner, x0, x1)
        tail = jnp.where(inner, x1, x2)
        for f in range(1, 4):
            x = tiles[4 * f : 4 * f + 4]
            x0 = lanes_left(x[a], b)
            x1 = lanes_left(x[a + 1], b) if a + 1 < 4 else x0
            rest = pltpu.roll(tail, NARROW - CHUNK * (f - 1), 1)
            out_ref[t, f] = jnp.where(lane < NARROW, jnp.where(inner, x0, x1), rest)


def put_state(ref, i, u, v):
    for at, x in ((0, u), (3, v)):
        ref[at, i] = x
        ref[at + 1, i] = pltpu.roll(x, 127, 1)
        ref[at + 2, i] = pltpu.roll(x, 1, 1)


def sweep(coef_ref, gu_ref, gv_ref, old, new, n, start):
    def west_side(i):
        return [old[k, i - 1] if i > 0 else pltpu.roll(old[k, n - 1], 1, 0) for k in range(6)]

    west = west_side(start)
    here = [old[k, start] for k in range(6)]
    for step in range(n):
        i = (start + step) % n
        if step and i == 0:
            west = west_side(0)
            here = [old[k, 0] for k in range(6)]
        east = [old[k, i + 1] if i < n - 1 else pltpu.roll(old[k, 0], 7, 0) for k in range(6)]
        half = coef_ref[0, i]
        fresh = []
        for own, other, base, source in ((0, 3, 1, gu_ref), (3, 0, 9, gv_ref)):
            c = [coef_ref[base + k, i] for k in range(8)]
            a = source[i] + half * here[own]
            b = c[0] * here[own + 1] + c[1] * here[own + 2]
            d = c[2] * east[own] + c[3] * west[own]
            e = c[4] * east[other + 1] + c[5] * west[other + 1]
            g = c[6] * east[other + 2] + c[7] * west[other + 2]
            fresh.append((a + b) + (d + (e + g)))
        put_state(new, i, *fresh)
        west, here = here, east


def sweeps(coef_ref, gu_ref, gv_ref, one, two, n):
    def body(_, carry):
        for k in range(UNROLL):
            old, new = (one, two) if k % 2 == 0 else (two, one)
            sweep(coef_ref, gu_ref, gv_ref, old, new, n, (n // 4 * k) % n)
        return carry

    lax.fori_loop(0, SWEEPS // UNROLL, body, 0)


def up_down():
    lane = lane_iota()
    up_ok = jnp.where(lane < 127, 1.0, 0.0).astype(F32)
    down_ok = jnp.where(lane > 0, 1.0, 0.0).astype(F32)
    return up_ok, down_ok, lambda x: pltpu.roll(x, 127, 1) * up_ok, lambda x: pltpu.roll(x, 1, 1) * down_ok


def east_of(ref, i):
    return ref[i + 1] if i < WB - 1 else pltpu.roll(ref[0], 7, 0)


def west_of(ref, i):
    return ref[i - 1] if i > 0 else pltpu.roll(ref[WB - 1], 1, 0)


def prepare_kernel(x_ref, blk, flat):
    def tile(k):
        return jnp.concatenate(
            [x_ref[t * PACK_ROWS + 8 * k : t * PACK_ROWS + 8 * k + 8, :] for t in range(N_TILE)], 0
        ).T

    for f in range(6):
        flat[f, 0:128, :] = tile(f)
    for k in range(3):
        tail = tile(6 + k)
        flat[2 * k, 128:WIDE, :] = tail[0:56]
        flat[2 * k + 1, 128:WIDE, :] = tail[56:112]
    for f in range(6):
        for i in range(WB):
            blk[f, i] = flat[f, pl.ds(i, 8, stride=WB), :]
    _, _, up, down = up_down()
    u_ref, v_ref = blk.at[0], blk.at[1]
    for i in range(WB):
        u, v = u_ref[i], v_ref[i]
        ux = 0.5 * (up(u) - down(u))
        vx = 0.5 * (up(v) - down(v))
        uy = 0.5 * (east_of(u_ref, i) - west_of(u_ref, i))
        vy = 0.5 * (east_of(v_ref, i) - west_of(v_ref, i))
        shear = uy + vx
        strain = ux * ux + vy * vy + ux * vy + 0.25 * shear * shear + REGULAR
        blk[6, i] = jnp.exp(jnp.log(strain) * (-1.0 / 3.0)) * (0.5 / LAYERS)


def solve_kernel(
    z_ref, blk, out_ref, flat, nu_ref, coef, wide_a, wide_b, tmp, near, near_a, near_b, gu_ref, gv_ref, turned
):
    def tile(k):
        return z_ref[:, k].reshape(128, 128).T

    flat[0, 0:128, :] = tile(0)
    for f in range(1, 4):
        size = min(CHUNK, WIDE - 128 - CHUNK * (f - 1))
        at = 128 + CHUNK * (f - 1)
        flat[0, at : at + size, :] = tile(f)[NARROW : NARROW + size]
    up_ok, down_ok, up, down = up_down()
    for i in range(WB):
        put_state(wide_a, i, blk[0, i], blk[1, i])
        nu_ref[i] = blk[6, i] * flat[0, pl.ds(i, 8, stride=WB), :]
    for i in range(WB):
        nu = nu_ref[i]
        nu_n, nu_s = up(nu), down(nu)
        nu_e, nu_w = east_of(nu_ref, i), west_of(nu_ref, i)
        drag, inside = blk[2, i], blk[3, i]
        n, s, e, w = 0.5 * (nu + nu_n), 0.5 * (nu + nu_s), 0.5 * (nu + nu_e), 0.5 * (nu + nu_w)
        rest = drag + 1.0 - inside
        q_u = 0.5 * inside / (4.0 * (n + s) + (e + w) + rest)
        q_v = 0.5 * inside / ((n + s) + 4.0 * (e + w) + rest)
        coef[0, i] = 0.5 * inside
        coef[1, i] = 4.0 * q_u * n * up_ok
        coef[2, i] = 4.0 * q_u * s * down_ok
        coef[3, i] = q_u * e
        coef[4, i] = q_u * w
        coef[5, i] = q_u * (0.5 * nu_n + 0.25 * nu_e) * up_ok
        coef[6, i] = -q_u * (0.5 * nu_n + 0.25 * nu_w) * up_ok
        coef[7, i] = -q_u * (0.5 * nu_s + 0.25 * nu_e) * down_ok
        coef[8, i] = q_u * (0.5 * nu_s + 0.25 * nu_w) * down_ok
        coef[9, i] = q_v * n * up_ok
        coef[10, i] = q_v * s * down_ok
        coef[11, i] = 4.0 * q_v * e
        coef[12, i] = 4.0 * q_v * w
        coef[13, i] = q_v * (0.5 * nu_e + 0.25 * nu_n) * up_ok
        coef[14, i] = -q_v * (0.5 * nu_w + 0.25 * nu_n) * up_ok
        coef[15, i] = -q_v * (0.5 * nu_e + 0.25 * nu_s) * down_ok
        coef[16, i] = q_v * (0.5 * nu_w + 0.25 * nu_s) * down_ok
        coef[17, i] = q_u * blk[4, i]
        coef[18, i] = q_v * blk[5, i]
        coef[19, i] = q_u
        coef[20, i] = q_v
    for k in range(19):
        j = k if k < 17 else k + 2
        for i in range(WB):
            tmp[k % 4, pl.ds(i, 8, stride=WB), :] = coef[j, i]
        for i in range(NB):
            near[k, i] = tmp[k % 4, pl.ds(SWEEPS + i, 8, stride=NB), :]
    sweeps(coef, coef.at[17], coef.at[18], wide_a, wide_b, WB)
    for i in range(WB):
        flat[0, pl.ds(i, 8, stride=WB), :] = wide_a[0, i]
        flat[1, pl.ds(i, 8, stride=WB), :] = wide_a[3, i]
        flat[2, pl.ds(i, 8, stride=WB), :] = blk[2, i]
    weight = tile(1)[0:NARROW]
    span = slice(SWEEPS, SWEEPS + NARROW)
    tmp[0, 0:NARROW, :] = weight * flat[0, span, :] - tile(2)[0:NARROW]
    tmp[1, 0:NARROW, :] = weight * flat[1, span, :] - tile(3)[0:NARROW]
    for i in range(NB):
        gu_ref[i] = near[17, i] * tmp[0, pl.ds(i, 8, stride=NB), :]
        gv_ref[i] = near[18, i] * tmp[1, pl.ds(i, 8, stride=NB), :]
        for k in range(6):
            near_a[k, i] = jnp.zeros((8, 128), F32)
    sweeps(near, gu_ref, gv_ref, near_a, near_b, NB)
    for i in range(NB):
        tmp[0, pl.ds(i, 8, stride=NB), :] = near_a[0, i]
        tmp[1, pl.ds(i, 8, stride=NB), :] = near_a[3, i]
    own = slice(2 * SWEEPS, 2 * SWEEPS + CHUNK)
    mine = slice(SWEEPS, SWEEPS + CHUNK)
    u, v, drag = flat[0, own, :], flat[1, own, :], flat[2, own, :]
    turned[0:CHUNK, :] = u
    turned[CHUNK : 2 * CHUNK, :] = v
    turned[2 * CHUNK : 3 * CHUNK, :] = -(drag * (u * tmp[0, mine, :] + v * tmp[1, mine, :]))
    turned[3 * CHUNK :, :] = jnp.zeros((128 - 3 * CHUNK, 128), F32)
    tmp[0, 0:128, :] = turned[...].T
    lane = lax.broadcasted_iota(jnp.int32, (N_TILE, 128), 1)
    pieces = [tmp[0, pl.ds(r, N_TILE, stride=8), :] for r in range(8)]
    for k in range(5):
        row = None
        for r in range(8):
            to = 3 * CHUNK * r - 128 * k
            if -3 * CHUNK < to < 128:
                piece = pltpu.roll(pieces[r], to % 128, 1) if to % 128 else pieces[r]
                row = piece if row is None else jnp.where(lane >= to, piece, row)
        for layer in range(N_LAYER):
            out_ref[pl.ds(5 * layer + k, N_TILE, stride=5 * N_LAYER), :] = row


def unpack_kernel(z_ref, vel_ref, grad_ref, rows_ref):
    lane = lane_iota()
    for group in range(N_TILE):
        for r in range(8):
            k, off = divmod(3 * CHUNK * r, 128)
            piece = lanes_left(z_ref[pl.ds(40 * group + k, 8, stride=5), :], off)
            if off + 3 * CHUNK > 128:
                more = lanes_left(z_ref[pl.ds(40 * group + k + 1, 8, stride=5), :], off)
                piece = jnp.where(lane < 128 - off, piece, more)
            rows_ref[pl.ds(64 * group + r, 8, stride=8), :] = piece
    for f in range(3):
        for j in range(TILES):
            tile = None
            for chunk in range(128 * j // CHUNK, (128 * j + 127) // CHUNK + 1):
                layer, t = divmod(chunk, N_TILE)
                to = CHUNK * chunk - 128 * j
                src = 8 * (t * N_LAYER + layer)
                piece = lanes_left(rows_ref[src : src + 8, :], CHUNK * f - to)
                tile = piece if tile is None else jnp.where(lane >= to, piece, tile)
            if f < 2:
                vel_ref[f, :, 128 * j : 128 * j + 128] = tile
            else:
                grad_ref[:, 128 * j : 128 * j + 128] = tile


VMEM = pl.BlockSpec(memory_space=pltpu.VMEM)
SMEM = pl.BlockSpec(memory_space=pltpu.SMEM)


def call(kernel, out_shapes, scratch=(), in_specs=None, flops=1000000, limit=8):
    return pl.pallas_call(
        kernel,
        out_shape=[jax.ShapeDtypeStruct(s, F32) for s in out_shapes],
        in_specs=in_specs,
        out_specs=[VMEM] * len(out_shapes),
        scratch_shapes=list(scratch),
        cost_estimate=pl.CostEstimate(flops=flops, bytes_accessed=1000000, transcendentals=0),
        compiler_params=pltpu.CompilerParams(vmem_limit_bytes=limit << 20),
    )


def exchange(x, axis):
    return lax.all_to_all(x, axis, split_axis=0, concat_axis=0, tiled=True)


def to_layers(own, other):
    moved = lax.ppermute(other, "layer", [(i, i ^ 1) for i in range(N_LAYER)])
    shape = own.shape[1:]
    blocks = call(add_kernel, [shape] * N_CHIP, in_specs=[VMEM] * 2)(own, moved)
    out = [blocks[0]]
    for d in range(1, N_CHIP):
        out.append(lax.ppermute(blocks[d], "layer", [(i, (i + 2 * d) % N_LAYER) for i in range(N_LAYER)]))
    return out


def on_device(
    velocity_guess, hardness, thickness, friction, grounded, ice_mask, driving,
    obs_cell, obs_east, obs_north, obs_weight, obs_count,
):
    slots = (N_TILE, BLOCK)
    me = lax.axis_index("layer").astype(jnp.int32).reshape(1)
    (packed,) = call(pack_kernel, [(N_TILE * PACK_ROWS, 128)], in_specs=[SMEM] * 2 + [VMEM] * 9, limit=58)(
        me, obs_count.reshape(1, N_TILE), obs_cell.reshape(slots), obs_east.reshape(slots),
        obs_north.reshape(slots), obs_weight.reshape(slots),
        velocity_guess, friction, grounded, ice_mask, driving,
    )
    arrived = exchange(packed.reshape(N_TILE, PACK_ROWS, 128), "tile").reshape(N_TILE * PACK_ROWS, 128)
    (stiff,) = call(stiffness_kernel, [(8, COLS)], in_specs=[VMEM] * 2)(hardness, thickness)
    parts = call(
        scatter_kernel,
        [(N_CHIP, 16, 8, 128)] * 2,
        scratch=[
            pltpu.VMEM((3 * PIECES * 96, DEPTH), jnp.bfloat16),
            pltpu.VMEM((256, DEPTH), jnp.bfloat16),
            pltpu.VMEM((3 * PIECES * 96, 256), F32),
            pltpu.VMEM((4, TILES + 2, 8, 128), F32),
        ],
        in_specs=[SMEM] + [VMEM] * 2,
        flops=3600000000,
        limit=16,
    )(me, arrived, stiff)
    parts = to_layers(*parts)
    (blocks,) = call(
        prepare_kernel, [(7, WB, 8, 128)], scratch=[pltpu.VMEM((6, WIDE, 128), F32)], in_specs=[VMEM]
    )(arrived)
    (chunks,) = call(chunks_kernel, [(N_TILE, 4, 8, 128)], in_specs=[VMEM] * N_CHIP)(*parts)
    chunks = exchange(chunks, "tile")
    (shares,) = call(
        solve_kernel,
        [(N_TILE * N_LAYER * 5, 128)],
        scratch=[
            pltpu.VMEM((3, WIDE, 128), F32),
            pltpu.VMEM((WB, 8, 128), F32),
            pltpu.VMEM((21, WB, 8, 128), F32),
            pltpu.VMEM((6, WB, 8, 128), F32),
            pltpu.VMEM((6, WB, 8, 128), F32),
            pltpu.VMEM((4, WIDE, 128), F32),
            pltpu.VMEM((19, NB, 8, 128), F32),
            pltpu.VMEM((6, NB, 8, 128), F32),
            pltpu.VMEM((6, NB, 8, 128), F32),
            pltpu.VMEM((NB, 8, 128), F32),
            pltpu.VMEM((NB, 8, 128), F32),
            pltpu.VMEM((128, 128), F32),
        ],
        in_specs=[VMEM] * 2,
        flops=3600000000,
        limit=16,
    )(chunks, blocks)
    shares = exchange(shares.reshape(N_TILE * N_LAYER * 5 * 128), ("tile", "layer"))
    velocity, gradient = call(
        unpack_kernel,
        [(2, 8, COLS), (8, COLS)],
        scratch=[pltpu.VMEM((N_TILE * N_LAYER * 8, 128), F32)],
        in_specs=[VMEM],
    )(shares.reshape(N_TILE * N_LAYER * 5, 128))
    return velocity, gradient


def solution(mesh):
    return jax.shard_map(
        on_device,
        mesh=mesh,
        in_specs=(
            P(None, "tile", None),
            P("layer", "tile", None),
            P("tile", None),
            P("tile", None),
            P("tile", None),
            P("tile", None),
            P(None, "tile", None),
            P("tile", "layer", None, None),
            P("tile", "layer", None, None),
            P("tile", "layer", None, None),
            P("tile", "layer", None, None),
            P("tile", "layer", None),
        ),
        out_specs=(P(None, "tile", None), P("tile", None)),
        check_vma=False,
    )
```

```python
import jax
import jax.numpy as jnp
from jax import lax
from jax.experimental import pallas as pl
from jax.experimental.pallas import tpu as pltpu
from jax.sharding import PartitionSpec as P

SWEEPS = 40
LAYERS = 32
REGULAR = 0.01

ROWS = 8
COLS = 3072
TILES = COLS // 128
N_TILE = 16
N_LAYER = 8
N_CHIP = N_LAYER // 2
BLOCK = 512
CHUNK = 24
WIDE = CHUNK + 4 * SWEEPS
NARROW = CHUNK + 2 * SWEEPS
WB = WIDE // 8
NB = NARROW // 8
SHARE = COLS // N_LAYER
F32 = jnp.float32
PACK_ROWS = 8 * 11
PIECES = 3
UNROLL = 20
DEPTH = 4096
OBS_ROWS = PACK_ROWS
OBS_AT = 72


def lane_iota():
    return lax.broadcasted_iota(jnp.int32, (8, 128), 1)


def lanes_left(x, by):
    by = by % 128
    return pltpu.roll(x, 128 - by, 1) if by else x


def pack_kernel(
    me_ref, count_ref, cell_ref, east_ref, north_ref, weight_ref,
    guess_ref, fric_ref, ground_ref, ice_ref, drive_ref, out_ref,
):
    row = lax.broadcasted_iota(jnp.int32, (N_TILE, BLOCK), 0)
    slot = lax.broadcasted_iota(jnp.int32, (N_TILE, BLOCK), 1)
    count = jnp.zeros((N_TILE, BLOCK), jnp.int32)
    for d in range(N_TILE):
        count = jnp.where(row == d, count_ref[0, d], count)
    weight = jnp.where(slot < count, weight_ref[...], 0.0)
    cell = cell_ref[...]
    high = cell >> 8
    strip_row = ((cell >> 10) * 11) >> 5
    place = ((high - strip_row * (COLS // 256)) * ROWS + strip_row) * 256 + (cell & 255)
    for f, x in enumerate((place.astype(F32), weight, weight * east_ref[...], weight * north_ref[...])):
        for k in range(4):
            for half in range(2):
                at = pl.ds(8 * half * PACK_ROWS + 8 * 9 + 4 * f + k, 8, stride=PACK_ROWS)
                out_ref[at, :] = x[8 * half : 8 * half + 8, 128 * k : 128 * k + 128]

    first = 3 * me_ref[0] - 1
    lane = lane_iota()
    fields = [[] for _ in range(6)]
    for k in range(5):
        g = first + k
        keep = jnp.where(jnp.logical_and(g >= 0, g < TILES), 1.0, 0.0).astype(F32)
        at = pl.ds(pl.multiple_of(jnp.clip(g, 0, TILES - 1) * 128, 128), 128)
        fields[0].append(guess_ref[0, :, at] * keep)
        fields[1].append(guess_ref[1, :, at] * keep)
        fields[2].append(fric_ref[:, at] * ground_ref[:, at].astype(F32) * keep)
        fields[3].append(ice_ref[:, at].astype(F32) * keep)
        fields[4].append(drive_ref[0, :, at] * keep)
        fields[5].append(drive_ref[1, :, at] * keep)
    for t in range(N_TILE):
        a, b = divmod(48 + CHUNK * t, 128)
        inner = lane < 128 - b
        tails = []
        for f in range(6):
            x0 = lanes_left(fields[f][a], b)
            x1 = lanes_left(fields[f][a + 1], b)
            x2 = lanes_left(fields[f][a + 2], b) if a + 2 < 5 else x1
            out_ref[t * PACK_ROWS + 8 * f : t * PACK_ROWS + 8 * f + 8, :] = jnp.where(inner, x0, x1)
            tails.append(jnp.where(inner, x1, x2))
        for k in range(3):
            at = t * PACK_ROWS + 8 * (6 + k)
            out_ref[at : at + 8, :] = jnp.where(lane < 56, tails[2 * k], pltpu.roll(tails[2 * k + 1], 56, 1))


def stiffness_kernel(hard_ref, thick_ref, out_ref):
    for g in range(TILES):
        at = slice(128 * g, 128 * g + 128)
        part = (hard_ref[0, :, at] + hard_ref[1, :, at]) + (hard_ref[2, :, at] + hard_ref[3, :, at])
        out_ref[:, at] = thick_ref[:, at] * part


def scatter_kernel(me_ref, obs_ref, stiff_ref, *refs):
    outs, (lhs_ref, rhs_ref, acc_ref, turned_ref) = refs[:2], refs[2:]
    acc_ref[...] = jnp.zeros_like(acc_ref)
    step16 = lax.broadcasted_iota(jnp.int32, (16, 128), 0).astype(F32).astype(jnp.bfloat16)
    zero16 = jnp.zeros((16, 128), jnp.bfloat16)
    one16 = jnp.ones((16, 128), jnp.bfloat16)

    def rows(x):
        return jnp.broadcast_to(x, (16, 128)).astype(jnp.bfloat16)

    def body(step, carry):
        for q in range(DEPTH // 128):
            lanes = slice(128 * q, 128 * q + 128)
            base = (step * (DEPTH // BLOCK) + q // 4) * OBS_ROWS + OBS_AT + q % 4
            place = obs_ref[pl.ds(base, 1), :].astype(jnp.int32)
            high = rows((place >> 8).astype(F32))
            low = rows((place & 255).astype(F32))
            pieces = []
            for f in range(3):
                value = obs_ref[pl.ds(base + 4 * (f + 1), 1), :]
                for k in range(PIECES):
                    piece = value.astype(jnp.bfloat16).astype(F32)
                    pieces.append(rows(piece))
                    if k < PIECES - 1:
                        value = value - piece
            for b in range(16):
                rhs_ref[16 * b : 16 * b + 16, lanes] = jnp.where(low == step16 + 16.0 * b, one16, zero16)
            for b in range(6):
                hit = high == step16 + 16.0 * b
                for k in range(3 * PIECES):
                    lhs_ref[k * 96 + 16 * b : k * 96 + 16 * b + 16, lanes] = jnp.where(hit, pieces[k], zero16)
        acc_ref[...] += lax.dot_general(
            lhs_ref[...], rhs_ref[...], (((1,), (1,)), ((), ())), preferred_element_type=F32
        )
        return carry

    lax.fori_loop(0, N_TILE * BLOCK // DEPTH, body, 0)
    lane = lane_iota()
    zero = jnp.zeros((8, 128), F32)

    def turn(f, tiles, shift):
        turned = [zero] + [lanes_left(x, shift) for x in tiles] + [zero, zero]
        for g in range(TILES + 2):
            turned_ref[f, g] = jnp.where(lane < 128 - shift, turned[g], turned[g + 1])

    turn(0, [stiff_ref[:, 128 * g : 128 * g + 128] for g in range(TILES)], 48)
    for f in range(3):
        total = acc_ref[PIECES * f * 96 : PIECES * f * 96 + 96, :]
        for k in range(1, PIECES):
            total = total + acc_ref[(PIECES * f + k) * 96 : (PIECES * f + k + 1) * 96, :]
        tiles = [total[8 * (g // 2) : 8 * (g // 2) + 8, 128 * (g % 2) : 128 * (g % 2) + 128] for g in range(TILES)]
        turn(f + 1, tiles, 88)
    chip, core = me_ref[0] >> 1, me_ref[0] & 1
    for side in range(2):
        for d in range(N_CHIP):
            first = 3 * (2 * ((chip + d) & (N_CHIP - 1)) + (core ^ side))
            for f in range(4):
                for k in range(4):
                    tile = turned_ref[f, first + k]
                    if f == 1 and k == 3:
                        tile = jnp.where(lane < 80, tile, pltpu.roll(turned_ref[0, first + 4], 80, 1))
                    outs[side][d, 4 * f + k] = tile


def add_kernel(a_ref, b_ref, *outs):
    for d in range(N_CHIP):
        outs[d][...] = a_ref[d] + b_ref[d]


def chunks_kernel(*refs):
    parts, out_ref = refs[:N_CHIP], refs[N_CHIP]
    lane = lane_iota()

    def summed(k):
        total = parts[0][k]
        for part in parts[1:]:
            total = total + part[k]
        return total

    tiles = [summed(k) for k in range(16)]
    stiff = tiles[0:4] + [lanes_left(tiles[7], 80)]
    for t in range(N_TILE):
        a, b = divmod(CHUNK * t, 128)
        inner = lane < 128 - b
        x0 = lanes_left(stiff[a], b)
        x1 = lanes_left(stiff[a + 1], b)
        x2 = lanes_left(stiff[a + 2], b) if a + 2 < 5 else x1
        out_ref[t, 0] = jnp.where(inner, x0, x1)
        tail = jnp.where(inner, x1, x2)
        for f in range(1, 4):
            x = tiles[4 * f : 4 * f + 4]
            x0 = lanes_left(x[a], b)
            x1 = lanes_left(x[a + 1], b) if a + 1 < 4 else x0
            rest = pltpu.roll(tail, NARROW - CHUNK * (f - 1), 1)
            out_ref[t, f] = jnp.where(lane < NARROW, jnp.where(inner, x0, x1), rest)


def put_state(ref, i, u, v):
    for at, x in ((0, u), (3, v)):
        ref[at, i] = x
        ref[at + 1, i] = pltpu.roll(x, 127, 1)
        ref[at + 2, i] = pltpu.roll(x, 1, 1)


def sweep(coef_ref, gu_ref, gv_ref, old, new, n, start):
    def west_side(i):
        return [old[k, i - 1] if i > 0 else pltpu.roll(old[k, n - 1], 1, 0) for k in range(6)]

    west = west_side(start)
    here = [old[k, start] for k in range(6)]
    for step in range(n):
        i = (start + step) % n
        if step and i == 0:
            west = west_side(0)
            here = [old[k, 0] for k in range(6)]
        east = [old[k, i + 1] if i < n - 1 else pltpu.roll(old[k, 0], 7, 0) for k in range(6)]
        half = coef_ref[0, i]
        fresh = []
        for own, other, base, source in ((0, 3, 1, gu_ref), (3, 0, 9, gv_ref)):
            c = [coef_ref[base + k, i] for k in range(8)]
            a = source[i] + half * here[own]
            b = c[0] * here[own + 1] + c[1] * here[own + 2]
            d = c[2] * east[own] + c[3] * west[own]
            e = c[4] * east[other + 1] + c[5] * west[other + 1]
            g = c[6] * east[other + 2] + c[7] * west[other + 2]
            fresh.append((a + b) + (d + (e + g)))
        put_state(new, i, *fresh)
        west, here = here, east


def sweeps(coef_ref, gu_ref, gv_ref, one, two, n):
    def body(_, carry):
        for k in range(UNROLL):
            old, new = (one, two) if k % 2 == 0 else (two, one)
            sweep(coef_ref, gu_ref, gv_ref, old, new, n, (n // 4 * k) % n)
        return carry

    lax.fori_loop(0, SWEEPS // UNROLL, body, 0)


def up_down():
    lane = lane_iota()
    up_ok = jnp.where(lane < 127, 1.0, 0.0).astype(F32)
    down_ok = jnp.where(lane > 0, 1.0, 0.0).astype(F32)
    return up_ok, down_ok, lambda x: pltpu.roll(x, 127, 1) * up_ok, lambda x: pltpu.roll(x, 1, 1) * down_ok


def east_of(ref, i):
    return ref[i + 1] if i < WB - 1 else pltpu.roll(ref[0], 7, 0)


def west_of(ref, i):
    return ref[i - 1] if i > 0 else pltpu.roll(ref[WB - 1], 1, 0)


def prepare_kernel(x_ref, blk, flat):
    def tile(k):
        return jnp.concatenate(
            [x_ref[t * PACK_ROWS + 8 * k : t * PACK_ROWS + 8 * k + 8, :] for t in range(N_TILE)], 0
        ).T

    for f in range(6):
        flat[f, 0:128, :] = tile(f)
    for k in range(3):
        tail = tile(6 + k)
        flat[2 * k, 128:WIDE, :] = tail[0:56]
        flat[2 * k + 1, 128:WIDE, :] = tail[56:112]
    for f in range(6):
        for i in range(WB):
            blk[f, i] = flat[f, pl.ds(i, 8, stride=WB), :]
    _, _, up, down = up_down()
    u_ref, v_ref = blk.at[0], blk.at[1]
    for i in range(WB):
        u, v = u_ref[i], v_ref[i]
        ux = 0.5 * (up(u) - down(u))
        vx = 0.5 * (up(v) - down(v))
        uy = 0.5 * (east_of(u_ref, i) - west_of(u_ref, i))
        vy = 0.5 * (east_of(v_ref, i) - west_of(v_ref, i))
        shear = uy + vx
        strain = ux * ux + vy * vy + ux * vy + 0.25 * shear * shear + REGULAR
        blk[6, i] = jnp.exp(jnp.log(strain) * (-1.0 / 3.0)) * (0.5 / LAYERS)


def solve_kernel(
    z_ref, blk, out_ref, flat, nu_ref, coef, wide_a, wide_b, tmp, near, near_a, near_b, gu_ref, gv_ref, turned
):
    def tile(k):
        return z_ref[:, k].reshape(128, 128).T

    flat[0, 0:128, :] = tile(0)
    for f in range(1, 4):
        size = min(CHUNK, WIDE - 128 - CHUNK * (f - 1))
        at = 128 + CHUNK * (f - 1)
        flat[0, at : at + size, :] = tile(f)[NARROW : NARROW + size]
    up_ok, down_ok, up, down = up_down()
    for i in range(WB):
        put_state(wide_a, i, blk[0, i], blk[1, i])
        nu_ref[i] = blk[6, i] * flat[0, pl.ds(i, 8, stride=WB), :]
    for i in range(WB):
        nu = nu_ref[i]
        nu_n, nu_s = up(nu), down(nu)
        nu_e, nu_w = east_of(nu_ref, i), west_of(nu_ref, i)
        drag, inside = blk[2, i], blk[3, i]
        n, s, e, w = 0.5 * (nu + nu_n), 0.5 * (nu + nu_s), 0.5 * (nu + nu_e), 0.5 * (nu + nu_w)
        rest = drag + 1.0 - inside
        q_u = 0.5 * inside / (4.0 * (n + s) + (e + w) + rest)
        q_v = 0.5 * inside / ((n + s) + 4.0 * (e + w) + rest)
        coef[0, i] = 0.5 * inside
        coef[1, i] = 4.0 * q_u * n * up_ok
        coef[2, i] = 4.0 * q_u * s * down_ok
        coef[3, i] = q_u * e
        coef[4, i] = q_u * w
        coef[5, i] = q_u * (0.5 * nu_n + 0.25 * nu_e) * up_ok
        coef[6, i] = -q_u * (0.5 * nu_n + 0.25 * nu_w) * up_ok
        coef[7, i] = -q_u * (0.5 * nu_s + 0.25 * nu_e) * down_ok
        coef[8, i] = q_u * (0.5 * nu_s + 0.25 * nu_w) * down_ok
        coef[9, i] = q_v * n * up_ok
        coef[10, i] = q_v * s * down_ok
        coef[11, i] = 4.0 * q_v * e
        coef[12, i] = 4.0 * q_v * w
        coef[13, i] = q_v * (0.5 * nu_e + 0.25 * nu_n) * up_ok
        coef[14, i] = -q_v * (0.5 * nu_w + 0.25 * nu_n) * up_ok
        coef[15, i] = -q_v * (0.5 * nu_e + 0.25 * nu_s) * down_ok
        coef[16, i] = q_v * (0.5 * nu_w + 0.25 * nu_s) * down_ok
        coef[17, i] = q_u * blk[4, i]
        coef[18, i] = q_v * blk[5, i]
        coef[19, i] = q_u
        coef[20, i] = q_v
    for k in range(19):
        j = k if k < 17 else k + 2
        for i in range(WB):
            tmp[k % 4, pl.ds(i, 8, stride=WB), :] = coef[j, i]
        for i in range(NB):
            near[k, i] = tmp[k % 4, pl.ds(SWEEPS + i, 8, stride=NB), :]
    sweeps(coef, coef.at[17], coef.at[18], wide_a, wide_b, WB)
    for i in range(WB):
        flat[0, pl.ds(i, 8, stride=WB), :] = wide_a[0, i]
        flat[1, pl.ds(i, 8, stride=WB), :] = wide_a[3, i]
        flat[2, pl.ds(i, 8, stride=WB), :] = blk[2, i]
    weight = tile(1)[0:NARROW]
    span = slice(SWEEPS, SWEEPS + NARROW)
    tmp[0, 0:NARROW, :] = weight * flat[0, span, :] - tile(2)[0:NARROW]
    tmp[1, 0:NARROW, :] = weight * flat[1, span, :] - tile(3)[0:NARROW]
    for i in range(NB):
        gu_ref[i] = near[17, i] * tmp[0, pl.ds(i, 8, stride=NB), :]
        gv_ref[i] = near[18, i] * tmp[1, pl.ds(i, 8, stride=NB), :]
        for k in range(6):
            near_a[k, i] = jnp.zeros((8, 128), F32)
    sweeps(near, gu_ref, gv_ref, near_a, near_b, NB)
    for i in range(NB):
        tmp[0, pl.ds(i, 8, stride=NB), :] = near_a[0, i]
        tmp[1, pl.ds(i, 8, stride=NB), :] = near_a[3, i]
    own = slice(2 * SWEEPS, 2 * SWEEPS + CHUNK)
    mine = slice(SWEEPS, SWEEPS + CHUNK)
    u, v, drag = flat[0, own, :], flat[1, own, :], flat[2, own, :]
    turned[0:CHUNK, :] = u
    turned[CHUNK : 2 * CHUNK, :] = v
    turned[2 * CHUNK : 3 * CHUNK, :] = -(drag * (u * tmp[0, mine, :] + v * tmp[1, mine, :]))
    turned[3 * CHUNK :, :] = jnp.zeros((128 - 3 * CHUNK, 128), F32)
    tmp[0, 0:128, :] = turned[...].T
    lane = lax.broadcasted_iota(jnp.int32, (N_TILE, 128), 1)
    pieces = [tmp[0, pl.ds(r, N_TILE, stride=8), :] for r in range(8)]
    for k in range(5):
        row = None
        for r in range(8):
            to = 3 * CHUNK * r - 128 * k
            if -3 * CHUNK < to < 128:
                piece = pltpu.roll(pieces[r], to % 128, 1) if to % 128 else pieces[r]
                row = piece if row is None else jnp.where(lane >= to, piece, row)
        for layer in range(N_LAYER):
            out_ref[pl.ds(5 * layer + k, N_TILE, stride=5 * N_LAYER), :] = row


def unpack_kernel(z_ref, vel_ref, grad_ref, rows_ref):
    lane = lane_iota()
    for group in range(N_TILE):
        for r in range(8):
            k, off = divmod(3 * CHUNK * r, 128)
            piece = lanes_left(z_ref[pl.ds(40 * group + k, 8, stride=5), :], off)
            if off + 3 * CHUNK > 128:
                more = lanes_left(z_ref[pl.ds(40 * group + k + 1, 8, stride=5), :], off)
                piece = jnp.where(lane < 128 - off, piece, more)
            rows_ref[pl.ds(64 * group + r, 8, stride=8), :] = piece
    for f in range(3):
        for j in range(TILES):
            tile = None
            for chunk in range(128 * j // CHUNK, (128 * j + 127) // CHUNK + 1):
                layer, t = divmod(chunk, N_TILE)
                to = CHUNK * chunk - 128 * j
                src = 8 * (t * N_LAYER + layer)
                piece = lanes_left(rows_ref[src : src + 8, :], CHUNK * f - to)
                tile = piece if tile is None else jnp.where(lane >= to, piece, tile)
            if f < 2:
                vel_ref[f, :, 128 * j : 128 * j + 128] = tile
            else:
                grad_ref[:, 128 * j : 128 * j + 128] = tile


VMEM = pl.BlockSpec(memory_space=pltpu.VMEM)
SMEM = pl.BlockSpec(memory_space=pltpu.SMEM)


def call(kernel, out_shapes, scratch=(), in_specs=None, flops=1000000, limit=8):
    return pl.pallas_call(
        kernel,
        out_shape=[jax.ShapeDtypeStruct(s, F32) for s in out_shapes],
        in_specs=in_specs,
        out_specs=[VMEM] * len(out_shapes),
        scratch_shapes=list(scratch),
        cost_estimate=pl.CostEstimate(flops=flops, bytes_accessed=1000000, transcendentals=0),
        compiler_params=pltpu.CompilerParams(vmem_limit_bytes=limit << 20),
    )


def exchange(x, axis):
    return lax.all_to_all(x, axis, split_axis=0, concat_axis=0, tiled=True)


def to_layers(own, other):
    moved = lax.ppermute(other, "layer", [(i, i ^ 1) for i in range(N_LAYER)])
    shape = own.shape[1:]
    blocks = call(add_kernel, [shape] * N_CHIP, in_specs=[VMEM] * 2)(own, moved)
    out = [blocks[0]]
    for d in range(1, N_CHIP):
        out.append(lax.ppermute(blocks[d], "layer", [(i, (i + 2 * d) % N_LAYER) for i in range(N_LAYER)]))
    return out


def on_device(
    velocity_guess, hardness, thickness, friction, grounded, ice_mask, driving,
    obs_cell, obs_east, obs_north, obs_weight, obs_count,
):
    slots = (N_TILE, BLOCK)
    me = lax.axis_index("layer").astype(jnp.int32).reshape(1)
    (packed,) = call(pack_kernel, [(N_TILE * PACK_ROWS, 128)], in_specs=[SMEM] * 2 + [VMEM] * 9, limit=58)(
        me, obs_count.reshape(1, N_TILE), obs_cell.reshape(slots), obs_east.reshape(slots),
        obs_north.reshape(slots), obs_weight.reshape(slots),
        velocity_guess, friction, grounded, ice_mask, driving,
    )
    arrived = exchange(packed.reshape(N_TILE, PACK_ROWS, 128), "tile").reshape(N_TILE * PACK_ROWS, 128)
    (stiff,) = call(stiffness_kernel, [(8, COLS)], in_specs=[VMEM] * 2)(hardness, thickness)
    parts = call(
        scatter_kernel,
        [(N_CHIP, 16, 8, 128)] * 2,
        scratch=[
            pltpu.VMEM((3 * PIECES * 96, DEPTH), jnp.bfloat16),
            pltpu.VMEM((256, DEPTH), jnp.bfloat16),
            pltpu.VMEM((3 * PIECES * 96, 256), F32),
            pltpu.VMEM((4, TILES + 2, 8, 128), F32),
        ],
        in_specs=[SMEM] + [VMEM] * 2,
        flops=3600000000,
        limit=24,
    )(me, arrived, stiff)
    parts = to_layers(*parts)
    (blocks,) = call(
        prepare_kernel, [(7, WB, 8, 128)], scratch=[pltpu.VMEM((6, WIDE, 128), F32)], in_specs=[VMEM]
    )(arrived)
    blocks, parts[0] = lax.optimization_barrier((blocks, parts[0]))
    (chunks,) = call(chunks_kernel, [(N_TILE, 4, 8, 128)], in_specs=[VMEM] * N_CHIP)(*parts)
    chunks = exchange(chunks, "tile")
    (shares,) = call(
        solve_kernel,
        [(N_TILE * N_LAYER * 5, 128)],
        scratch=[
            pltpu.VMEM((3, WIDE, 128), F32),
            pltpu.VMEM((WB, 8, 128), F32),
            pltpu.VMEM((21, WB, 8, 128), F32),
            pltpu.VMEM((6, WB, 8, 128), F32),
            pltpu.VMEM((6, WB, 8, 128), F32),
            pltpu.VMEM((4, WIDE, 128), F32),
            pltpu.VMEM((19, NB, 8, 128), F32),
            pltpu.VMEM((6, NB, 8, 128), F32),
            pltpu.VMEM((6, NB, 8, 128), F32),
            pltpu.VMEM((NB, 8, 128), F32),
            pltpu.VMEM((NB, 8, 128), F32),
            pltpu.VMEM((128, 128), F32),
        ],
        in_specs=[VMEM] * 2,
        flops=3600000000,
        limit=16,
    )(chunks, blocks)
    shares = exchange(shares.reshape(N_TILE * N_LAYER * 5 * 128), ("tile", "layer"))
    velocity, gradient = call(
        unpack_kernel,
        [(2, 8, COLS), (8, COLS)],
        scratch=[pltpu.VMEM((N_TILE * N_LAYER * 8, 128), F32)],
        in_specs=[VMEM],
    )(shares.reshape(N_TILE * N_LAYER * 5, 128))
    return velocity, gradient


def solution(mesh):
    return jax.shard_map(
        on_device,
        mesh=mesh,
        in_specs=(
            P(None, "tile", None),
            P("layer", "tile", None),
            P("tile", None),
            P("tile", None),
            P("tile", None),
            P("tile", None),
            P(None, "tile", None),
            P("tile", "layer", None, None),
            P("tile", "layer", None, None),
            P("tile", "layer", None, None),
            P("tile", "layer", None, None),
            P("tile", "layer", None),
        ),
        out_specs=(P(None, "tile", None), P("tile", None)),
        check_vma=False,
    )
```
